256 devices in a mesh: sy: 8 (over x_hi, y), sx: 2 (over core), grp: 16 (over z, x_lo).
Axes of the slice: x: 4 (x_hi: 2, x_lo: 2; x = x_hi * 2 + x_lo), y: 4, z: 8, core: 2. Of those that a mesh axis runs over, the one named last changes fastest.
Arguments:
- image: bfloat16 [16, 64, 256, 256], P('grp', None, 'sy', 'sx'), may hold values from -6 to 6
- weight_one: bfloat16 [3, 3, 64, 64], replicated, may hold values from -0.25 to 0.25
- bias_one: float32 [64], replicated, may hold values from -3 to 3
- weight_two: bfloat16 [3, 3, 64, 64], replicated, may hold values from -0.25 to 0.25
- bias_two: float32 [64], replicated, may hold values from -3 to 3
- cotangent: bfloat16 [16, 64, 256, 256], P('grp', None, 'sy', 'sx'), may hold values from -51 to 51
Outputs:
- output: bfloat16 [16, 64, 256, 256], P('grp', None, 'sy', 'sx')
- image_grad: bfloat16 [16, 64, 256, 256], P('grp', None, 'sy', 'sx')
- grad_weight_one: float32 [3, 3, 64, 64], replicated
- grad_bias_one: float32 [64], replicated
- grad_weight_two: float32 [3, 3, 64, 64], replicated
- grad_bias_two: float32 [64], replicated
The draws below stay inside these ranges and needn't reach their ends.
All inputs are finite; a program needn't handle non-finite values.
Results may differ from the reference program's by a relative error of at most 0.0075.
Values may be sent and summed in bfloat16 or wider, within the bound.
A program may use at most 64 MiB of HBM per device.

```python
import math
import jax
import jax.numpy as jnp
from jax import lax

C = 64
SLIDES = 16
NH = 256
NW = 256


def draw_cotangent(key, part):
    keys = jax.random.split(key, 3)
    shape = (SLIDES, C, NH, NW)
    base = jax.random.truncated_normal(keys[0], -4.0, 4.0, shape, jnp.float32)
    row_scale = jnp.exp(jax.random.uniform(keys[1], (SLIDES, 1, NH, 1), jnp.float32) * (0.5 * math.log(10.0)))
    col_scale = jnp.exp(jax.random.uniform(keys[2], (SLIDES, 1, 1, NW), jnp.float32) * (0.5 * math.log(10.0)))
    rising = 1.0 + 2.0 * jnp.arange(SLIDES, dtype=jnp.float32).reshape(SLIDES, 1, 1, 1) / max(SLIDES - 1, 1)
    return (0.3 * base * row_scale * col_scale * rising).astype(jnp.bfloat16)


def level_of(stream_key, extent, pieces, smallest, high):
    loudness, own = 1.0, jax.random.fold_in(stream_key, 6)
    for dim, parts in pieces:
        heights = jnp.exp(jax.random.uniform(jax.random.fold_in(own, dim), (parts,), jnp.float32, smallest / len(pieces), high / len(pieces)))
        loudness = loudness * jnp.repeat(heights, extent[dim] // parts).reshape([-1 if axis == dim else 1 for axis in range(len(extent))])
    return loudness


def scatter_about(rng, shape, deviation, limit, shards=(), kind=jnp.bfloat16):
    values = deviation * jax.random.normal(rng, shape, jnp.float32)
    if shards:
        values = values * level_of(rng, shape, shards, -0.22, 0.18)
    return jnp.clip(values, -limit, limit).astype(kind)


def setup_inputs(seed: int = 0) -> dict:
    key_of = jax.random.split(jax.random.key(seed), 7)
    image = scatter_about(key_of[0], (SLIDES, C, NH, NW), 1.0, 6.0, ((0, 16), (2, 8), (3, 2)))
    weight_one = scatter_about(key_of[1], (3, 3, C, C), (9 * C) ** -0.5, 0.25)
    bias_one = scatter_about(key_of[2], (C,), 0.5, 3.0, (), jnp.float32)
    weight_two = scatter_about(key_of[3], (3, 3, C, C), (9 * C) ** -0.5, 0.25)
    bias_two = scatter_about(key_of[4], (C,), 0.5, 3.0, (), jnp.float32)
    cotangent = draw_cotangent(jax.random.fold_in(key_of[6], 71), 0)
    return {"image": image, "weight_one": weight_one, "bias_one": bias_one, "weight_two": weight_two, "bias_two": bias_two, "cotangent": cotangent}


def convolve(padded, kernel):
    return lax.conv_general_dilated(padded, kernel, (1, 1), 'VALID', dimension_numbers=('NCHW', 'HWIO', 'NCHW'), preferred_element_type=jnp.float32)

def flipped(kernel):
    return jnp.transpose(kernel[::-1, ::-1], (0, 1, 3, 2))

def pad_edges(field):
    return jnp.pad(field, ((0, 0), (0, 0), (1, 1), (1, 1)))

def kernel_grad(padded, delta):
    rows = delta.shape[2]
    cols = delta.shape[3]
    taps = []
    for row_tap in range(3):
        for col_tap in range(3):
            window = padded[0, :, row_tap:row_tap + rows, col_tap:col_tap + cols].astype(jnp.float32)
            taps.append(jnp.einsum('ihw,ohw->io', window, delta[0].astype(jnp.float32)))
    return jnp.stack(taps).reshape(3, 3, delta.shape[1], delta.shape[1])

def slope(pre):
    gate = jax.nn.sigmoid(pre)
    return gate * (1.0 + pre * (1.0 - gate))

def one_slide(image, cotangent, weight_one, bias_one, weight_two, bias_two):
    image_pad = pad_edges(image[None])
    pre_one = convolve(image_pad, weight_one) + bias_one.reshape(1, -1, 1, 1)
    hidden = (pre_one * jax.nn.sigmoid(pre_one)).astype(jnp.bfloat16)
    hidden_pad = pad_edges(hidden)
    pre_two = convolve(hidden_pad, weight_two) + bias_two.reshape(1, -1, 1, 1)
    output = (pre_two * jax.nn.sigmoid(pre_two)).astype(jnp.bfloat16)
    delta_two = (cotangent[None].astype(jnp.float32) * slope(pre_two)).astype(jnp.bfloat16)
    grad_two = kernel_grad(hidden_pad, delta_two)
    bias_grad_two = lax.optimization_barrier(jnp.sum(delta_two.astype(jnp.float32), axis=(0, 2, 3)))
    hidden_grad = convolve(pad_edges(delta_two), flipped(weight_two))
    delta_one = (hidden_grad * slope(pre_one)).astype(jnp.bfloat16)
    grad_one = kernel_grad(image_pad, delta_one)
    bias_grad_one = lax.optimization_barrier(jnp.sum(delta_one.astype(jnp.float32), axis=(0, 2, 3)))
    image_grad = convolve(pad_edges(delta_one), flipped(weight_one)).astype(jnp.bfloat16)
    return (output[0], image_grad[0], grad_one, bias_grad_one, grad_two, bias_grad_two)

def reference(image, weight_one, bias_one, weight_two, bias_two, cotangent):

    def per_slide(pair):
        return one_slide(pair[0], pair[1], weight_one, bias_one, weight_two, bias_two)
    results = lax.map(per_slide, (image, cotangent))
    factor = (SLIDES * NH * NW) ** (-0.5)
    return (results[0], results[1], lax.optimization_barrier(jnp.sum(results[2], axis=0)) * factor, lax.optimization_barrier(jnp.sum(results[3], axis=0)) * factor, lax.optimization_barrier(jnp.sum(results[4], axis=0)) * factor, lax.optimization_barrier(jnp.sum(results[5], axis=0)) * factor)
```

```python
import functools

import jax
import jax.numpy as jnp
from jax import lax
from jax.experimental import pallas as pl
from jax.experimental.pallas import tpu as pltpu
from jax.sharding import PartitionSpec as P

BF = jnp.bfloat16
F32 = jnp.float32
MESH = pl.DeviceIdType.MESH
CH = 64
RB = 32
CB = 128
RW = 16
CW = 256
FLAT = 289


def sigmoid(x):
    return 0.5 * jnp.tanh(0.5 * x) + 0.5


def store_shifted(x, dst, r, lane):
    z = jnp.zeros_like(x)
    dst[r, 0:CH] = jnp.where(lane == 0, z, pltpu.roll(x, 1, 1))
    dst[r, CH : 2 * CH] = x
    dst[r, 2 * CH : 3 * CH] = jnp.where(lane == CW - 1, z, pltpu.roll(x, CW - 1, 1))


def build_weights(w_ref, dst, transposed):
    dst[...] = jnp.zeros_like(dst)
    for a in range(3):
        for b in range(3):
            if transposed:
                block = w_ref[2 - a, 2 - b]
            else:
                block = w_ref[a, b].astype(F32).T.astype(BF)
            for t in range(2):
                first = (a + t) * 3 * CH + b * CH
                dst[t * CH : (t + 1) * CH, first : first + CH] = block


def conv(w, src, k):
    rhs = src[pl.ds(2 * k, 4)].reshape(4 * 3 * CH, CW)
    return jnp.dot(w[...], rhs, preferred_element_type=F32)


def kernel(
    n_sy,
    n_grp,
    scale,
    x_ref,
    ct_ref,
    w1_ref,
    b1_ref,
    w2_ref,
    b2_ref,
    out_ref,
    ig_ref,
    g1_ref,
    gb1_ref,
    g2_ref,
    gb2_ref,
    turn,
    xt,
    ctt,
    xw,
    ctw,
    x3,
    h3,
    d3,
    e3,
    s1,
    dz,
    w1t,
    w2t,
    w1f,
    w2f,
    outw,
    igw,
    outs,
    igs,
    gacc,
    flat,
    part2,
    part1,
    in2,
    in1,
    mid2,
    mid1,
    fin2,
    fin1,
    send_halo,
    recv_halo,
    send_red,
    recv_red,
):
    sy = lax.axis_index("sy")
    sx = lax.axis_index("sx")
    grp = lax.axis_index("grp")
    n_m = 2 * n_sy
    m = sy * 2 + sx
    chunk = part1.shape[1]

    barrier = pltpu.get_barrier_semaphore()

    @pl.loop(1, n_m)
    def _(d):
        peer = lax.rem(m + d, n_m)
        pl.semaphore_signal(
            barrier,
            inc=1,
            device_id={"sy": peer // 2, "sx": lax.rem(peer, 2)},
            device_id_type=MESH,
        )

    @pl.loop(1, n_grp)
    def _(d):
        pl.semaphore_signal(
            barrier, inc=1, device_id={"grp": lax.rem(grp + d, n_grp)}, device_id_type=MESH
        )

    lane = lax.broadcasted_iota(jnp.int32, (CH, CW), 1)
    mine = pl.multiple_of(sx * CB, CB)
    other = pl.multiple_of((1 - sx) * CB, CB)

    def rows_major(src, dst):
        @pl.loop(0, 8)
        def _(c):
            part = src[pl.ds(8 * c, 8)].astype(F32).reshape(8 * RB, CB)
            turn[pl.ds(pl.multiple_of(8 * RB * c, 8 * RB), 8 * RB)] = part

        @pl.loop(0, RB)
        def _(r):
            dst[r] = turn[pl.ds(r, CH, stride=RB), :].astype(BF)

    def halo_copies(i, blk, win, width):
        span = RW + width
        near = pltpu.make_async_copy(
            blk.at[pl.ds(sx * (RW - width), span)],
            win.at[pl.ds((1 - sx) * width, span), :, pl.ds(mine, CB)],
            send_halo.at[i, 0],
        )
        pair = pltpu.make_async_remote_copy(
            src_ref=blk.at[pl.ds((1 - sx) * (RW - width), span)],
            dst_ref=win.at[pl.ds(sx * width, span), :, pl.ds(mine, CB)],
            send_sem=send_halo.at[i, 1],
            recv_sem=recv_halo.at[i, 0],
            device_id={"sx": 1 - sx},
            device_id_type=MESH,
        )
        down = pltpu.make_async_remote_copy(
            src_ref=blk.at[pl.ds(RB - width, width)],
            dst_ref=win.at[pl.ds(0, width), :, pl.ds(mine, CB)],
            send_sem=send_halo.at[i, 2],
            recv_sem=recv_halo.at[i, 1 + sx],
            device_id={"sy": sy + 1, "sx": 0},
            device_id_type=MESH,
        )
        up = pltpu.make_async_remote_copy(
            src_ref=blk.at[pl.ds(0, width)],
            dst_ref=win.at[pl.ds(RW + width, width), :, pl.ds(mine, CB)],
            send_sem=send_halo.at[i, 3],
            recv_sem=recv_halo.at[i, 1 + sx],
            device_id={"sy": sy - 1, "sx": 1},
            device_id_type=MESH,
        )
        return near, pair, down, up

    has_down = sy < n_sy - 1
    has_up = sy > 0
    takes = ((sx == 0) & has_up) | ((sx == 1) & has_down)

    def halo_start(i, blk, win, width):
        near, pair, down, up = halo_copies(i, blk, win, width)
        near.start()
        pair.start()
        pl.when(has_down)(down.start)
        pl.when(has_up)(up.start)
        empty = jnp.zeros((width, CH, CW), BF)

        @pl.when((sx == 0) & (sy == 0))
        def _():
            win[0:width] = empty

        @pl.when((sx == 1) & (sy == n_sy - 1))
        def _():
            win[RW + width : RW + 2 * width] = empty

    def halo_wait(i, blk, win, width):
        near, pair, down, up = halo_copies(i, blk, win, width)
        near.wait()
        pair.wait()
        pl.when(has_down)(down.wait_send)
        pl.when(has_up)(up.wait_send)

        @pl.when(takes)
        def _():
            for half in range(2):
                pltpu.make_async_remote_copy(
                    src_ref=blk.at[pl.ds(0, width)],
                    dst_ref=win.at[
                        pl.ds(sx * (RW + width), width), :, half * CB : (half + 1) * CB
                    ],
                    send_sem=send_halo.at[i, 2],
                    recv_sem=recv_halo.at[i, 1 + half],
                    device_id={"sx": 1 - sx},
                    device_id_type=MESH,
                ).wait_recv()

    rows_major(x_ref, xt)
    pl.semaphore_wait(barrier, n_m - 1 + n_grp - 1)
    halo_start(0, xt, xw, 4)
    rows_major(ct_ref, ctt)
    halo_start(1, ctt, ctw, 2)

    build_weights(w1_ref, w1t, False)
    build_weights(w2_ref, w2t, False)
    build_weights(w1_ref, w1f, True)
    build_weights(w2_ref, w2f, True)
    b1 = jnp.broadcast_to(b1_ref[...], (CH, CW))
    b2 = jnp.broadcast_to(b2_ref[...], (CH, CW))
    b1 = jnp.concatenate([b1, b1], 0)
    b2 = jnp.concatenate([b2, b2], 0)
    blank = jnp.zeros((CH, CW), BF)
    for r in (0, 1, RW + 2, RW + 3):
        dz[r] = blank
    first = (sx == 0) & (sy == 0)
    last = (sx == 1) & (sy == n_sy - 1)

    halo_wait(0, xt, xw, 4)

    @pl.loop(0, RW + 8)
    def _(r):
        store_shifted(xw[r], x3, r, lane)

    @pl.loop(0, (RW + 6) // 2)
    def _(k):
        pre = conv(w1t, x3, k) + b1
        gate = sigmoid(pre)
        h = (pre * gate).astype(BF)
        s1[pl.ds(2 * k, 2)] = (gate * (1.0 + pre * (1.0 - gate))).reshape(2, CH, CW)
        store_shifted(h[0:CH], h3, 2 * k, lane)
        store_shifted(h[CH : 2 * CH], h3, 2 * k + 1, lane)

    @pl.when(first)
    def _():
        h3[0:3] = jnp.zeros((3, 3 * CH, CW), BF)

    @pl.when(last)
    def _():
        h3[RW + 3 : RW + 6] = jnp.zeros((3, 3 * CH, CW), BF)

    halo_wait(1, ctt, ctw, 2)

    @pl.loop(0, (RW + 4) // 2)
    def _(k):
        pre = conv(w2t, h3, k) + b2
        gate = sigmoid(pre)
        slope = gate * (1.0 + pre * (1.0 - gate))
        ct = ctw[pl.ds(2 * k, 2)].reshape(2 * CH, CW)
        d = (ct.astype(F32) * slope).astype(BF)
        store_shifted(d[0:CH], d3, 2 * k, lane)
        store_shifted(d[CH : 2 * CH], d3, 2 * k + 1, lane)

        @pl.when((k > 0) & (k < (RW + 4) // 2 - 1))
        def _():
            outw[pl.ds(2 * k - 2, 2)] = (pre * gate).astype(BF).reshape(2, CH, CW)
            dz[pl.ds(2 * k, 2)] = d.reshape(2, CH, CW)

    def pair_copy(i, src, dst):
        return pltpu.make_async_remote_copy(
            src_ref=src.at[:, :, pl.ds(other, CB)],
            dst_ref=dst,
            send_sem=send_halo.at[2 + i, 0],
            recv_sem=recv_halo.at[2 + i, 0],
            device_id={"sx": 1 - sx},
            device_id_type=MESH,
        )

    pair_copy(0, outw, outs).start()

    def kernel_grad(src, off, dst):
        gacc[...] = jnp.zeros_like(gacc)
        ones = jnp.ones((16, CW), BF)

        @pl.loop(0, (RW + 2) // 2)
        def _(k):
            q = 2 * k
            left = [jnp.concatenate([src[q + j + off], ones], 0) for j in range(2)]
            right = [dz[pl.ds(q + j, 3)].reshape(3 * CH, CW) for j in range(2)]
            gacc[...] += lax.dot_general(
                jnp.concatenate(left, 1),
                jnp.concatenate(right, 1),
                (((1,), (1,)), ((), ())),
                preferred_element_type=F32,
            )

        flat[0:192] = gacc[0:192, 0:128]
        tail = gacc[0:192, 128:192]
        flat[192:288] = jnp.concatenate([tail[0:96], tail[96:192]], 1)
        flat[288:289] = gacc[192:193, 0:128]
        for j in range(n_m):
            top = min(FLAT, (j + 1) * chunk)
            if top > j * chunk:
                dst[j, 0 : top - j * chunk] = flat[j * chunk : top]

    def peer_of(d):
        peer = lax.rem(m + d, n_m)
        return peer, {"sy": peer // 2, "sx": lax.rem(peer, 2)}

    def scatter(i, part, landing):
        def copy(d):
            peer, where = peer_of(d)
            return pltpu.make_async_remote_copy(
                src_ref=part.at[peer],
                dst_ref=landing.at[m],
                send_sem=send_red.at[i, d],
                recv_sem=recv_red.at[i, m],
                device_id=where,
                device_id_type=MESH,
            )

        return copy

    def across(i, mid):
        def copy(d):
            return pltpu.make_async_remote_copy(
                src_ref=mid.at[grp],
                dst_ref=mid.at[grp],
                send_sem=send_red.at[i, d],
                recv_sem=recv_red.at[i, grp],
                device_id={"grp": lax.rem(grp + d, n_grp)},
                device_id_type=MESH,
            )

        return copy

    def gather(i, fin):
        def copy(d):
            _, where = peer_of(d)
            return pltpu.make_async_remote_copy(
                src_ref=fin.at[m],
                dst_ref=fin.at[m],
                send_sem=send_red.at[i, d],
                recv_sem=recv_red.at[i, m],
                device_id=where,
                device_id_type=MESH,
            )

        return copy

    def start_all(copy, count):
        @pl.loop(1, count)
        def _(d):
            copy(d).start()

    def wait_all(copy, i, count, me, landing):
        @pl.loop(1, count)
        def _(d):
            slot = lax.rem(me + d, count)
            copy(d).wait_send()
            pltpu.make_async_remote_copy(
                src_ref=landing.at[slot],
                dst_ref=landing.at[slot],
                send_sem=send_red.at[i, d],
                recv_sem=recv_red.at[i, slot],
                device_id={"sx": 1 - sx},
                device_id_type=MESH,
            ).wait_recv()

    def total(landing, count):
        acc = landing[0]
        for j in range(1, count):
            acc = acc + landing[j]
        return acc

    def step_scatter(i, part, landing):
        landing[m] = part[m]
        start_all(scatter(i, part, landing), n_m)

    def step_across(i, part, landing, mid):
        wait_all(scatter(i, part, landing), i, n_m, m, landing)
        mid[grp] = total(landing, n_m)
        start_all(across(i + 1, mid), n_grp)

    def step_gather(i, mid, fin):
        wait_all(across(i + 1, mid), i + 1, n_grp, grp, mid)
        fin[m] = total(mid, n_grp)
        start_all(gather(i + 2, fin), n_m)

    def step_end(i, fin, g_out, gb_out):
        wait_all(gather(i + 2, fin), i + 2, n_m, m, fin)
        for j in range(n_m):
            top = min(FLAT, (j + 1) * chunk)
            if top > j * chunk:
                flat[j * chunk : top] = fin[j, 0 : top - j * chunk] * scale
        wide = flat[0:192]
        g_out[2] = wide[:, 0:64]
        g_out[1] = wide[:, 64:128]
        tail = flat[192:288]
        g_out[0, 0:96] = tail[:, 0:64]
        g_out[0, 96:192] = tail[:, 64:128]
        gb_out[...] = flat[288:289, 0:64]

    kernel_grad(h3, 2, part2)
    step_scatter(0, part2, in2)

    @pl.loop(0, (RW + 2) // 2)
    def _(k):
        hg = conv(w2f, d3, k)
        d = (hg * s1[pl.ds(2 * k + 2, 2)].reshape(2 * CH, CW)).astype(BF)
        top, low = d[0:CH], d[CH : 2 * CH]
        store_shifted(top, e3, 2 * k, lane)
        store_shifted(low, e3, 2 * k + 1, lane)
        dz[2 * k + 1] = top
        dz[2 * k + 2] = low

    dz[1] = blank
    dz[RW + 2] = blank

    @pl.when(first)
    def _():
        e3[0] = jnp.zeros((3 * CH, CW), BF)

    @pl.when(last)
    def _():
        e3[RW + 1] = jnp.zeros((3 * CH, CW), BF)

    kernel_grad(x3, 3, part1)
    step_scatter(3, part1, in1)
    step_across(0, part2, in2, mid2)

    @pl.loop(0, RW // 2)
    def _(k):
        igw[pl.ds(2 * k, 2)] = conv(w1f, e3, k).astype(BF).reshape(2, CH, CW)

    pair_copy(1, igw, igs).start()
    step_across(3, part1, in1, mid1)
    step_gather(0, mid2, fin2)

    def channels_major(i, own, got, dst):
        pair_copy(i, own, got).wait()

        @pl.loop(0, RW)
        def _(r):
            turn[pl.ds(sx * RW + r, CH, stride=RB), :] = own[r, :, pl.ds(mine, CB)].astype(F32)
            turn[pl.ds((1 - sx) * RW + r, CH, stride=RB), :] = got[r].astype(F32)

        @pl.loop(0, 8)
        def _(c):
            part = turn[pl.ds(pl.multiple_of(8 * RB * c, 8 * RB), 8 * RB)]
            dst[pl.ds(8 * c, 8)] = part.reshape(8, RB, CB).astype(BF)

    channels_major(0, outw, outs, out_ref)
    channels_major(1, igw, igs, ig_ref)
    step_gather(3, mid1, fin1)
    step_end(0, fin2, g2_ref, gb2_ref)
    step_end(3, fin1, g1_ref, gb1_ref)


def solution(mesh):
    n_sy = mesh.shape["sy"]
    n_grp = mesh.shape["grp"]
    n_m = 2 * n_sy
    chunk = -(-FLAT // n_m)
    scale = float((n_grp * n_sy * RB * 2 * CB) ** -0.5)
    most = max(n_m, n_grp)
    call = pl.pallas_call(
        functools.partial(kernel, n_sy, n_grp, scale),
        out_shape=[
            jax.ShapeDtypeStruct((CH, RB, CB), BF),
            jax.ShapeDtypeStruct((CH, RB, CB), BF),
            jax.ShapeDtypeStruct((3, 3 * CH, CH), F32),
            jax.ShapeDtypeStruct((1, CH), F32),
            jax.ShapeDtypeStruct((3, 3 * CH, CH), F32),
            jax.ShapeDtypeStruct((1, CH), F32),
        ],
        in_specs=[pl.BlockSpec(memory_space=pltpu.VMEM)] * 6,
        out_specs=[pl.BlockSpec(memory_space=pltpu.VMEM)] * 6,
        scratch_shapes=[
            pltpu.VMEM((CH * RB, CB), F32),
            pltpu.VMEM((RB, CH, CB), BF),
            pltpu.VMEM((RB, CH, CB), BF),
            pltpu.VMEM((RW + 8, CH, CW), BF),
            pltpu.VMEM((RW + 4, CH, CW), BF),
            pltpu.VMEM((RW + 8, 3 * CH, CW), BF),
            pltpu.VMEM((RW + 6, 3 * CH, CW), BF),
            pltpu.VMEM((RW + 4, 3 * CH, CW), BF),
            pltpu.VMEM((RW + 2, 3 * CH, CW), BF),
            pltpu.VMEM((RW + 6, CH, CW), F32),
            pltpu.VMEM((RW + 4, CH, CW), BF),
            pltpu.VMEM((2 * CH, 12 * CH), BF),
            pltpu.VMEM((2 * CH, 12 * CH), BF),
            pltpu.VMEM((2 * CH, 12 * CH), BF),
            pltpu.VMEM((2 * CH, 12 * CH), BF),
            pltpu.VMEM((RW, CH, CW), BF),
            pltpu.VMEM((RW, CH, CW), BF),
            pltpu.VMEM((RW, CH, CB), BF),
            pltpu.VMEM((RW, CH, CB), BF),
            pltpu.VMEM((208, 192), F32),
            pltpu.VMEM((FLAT, 128), F32),
            pltpu.VMEM((n_m, chunk, 128), F32),
            pltpu.VMEM((n_m, chunk, 128), F32),
            pltpu.VMEM((n_m, chunk, 128), F32),
            pltpu.VMEM((n_m, chunk, 128), F32),
            pltpu.VMEM((n_grp, chunk, 128), F32),
            pltpu.VMEM((n_grp, chunk, 128), F32),
            pltpu.VMEM((n_m, chunk, 128), F32),
            pltpu.VMEM((n_m, chunk, 128), F32),
            pltpu.SemaphoreType.DMA((4, 4)),
            pltpu.SemaphoreType.DMA((4, 3)),
            pltpu.SemaphoreType.DMA((6, most)),
            pltpu.SemaphoreType.DMA((6, most)),
        ],
        compiler_params=pltpu.CompilerParams(
            collective_id=0, has_side_effects=True, vmem_limit_bytes=50 * 1024 * 1024
        ),
        name="blocks",
    )

    def local(image, weight_one, bias_one, weight_two, bias_two, cotangent):
        output, image_grad, g1, gb1, g2, gb2 = call(
            image[0],
            cotangent[0],
            weight_one,
            bias_one.reshape(CH, 1),
            weight_two,
            bias_two.reshape(CH, 1),
        )
        return (
            output[None],
            image_grad[None],
            g1.reshape(3, 3, CH, CH),
            gb1.reshape(CH),
            g2.reshape(3, 3, CH, CH),
            gb2.reshape(CH),
        )

    tile = P("grp", None, "sy", "sx")
    return jax.shard_map(
        local,
        mesh=mesh,
        in_specs=(tile, P(), P(), P(), P(), tile),
        out_specs=(tile, tile, P(), P(), P(), P()),
        check_vma=False,
    )
```

```python
import functools

import jax
import jax.numpy as jnp
from jax import lax
from jax.experimental import pallas as pl
from jax.experimental.pallas import tpu as pltpu
from jax.sharding import PartitionSpec as P

BF = jnp.bfloat16
F32 = jnp.float32
MESH = pl.DeviceIdType.MESH
CH = 64
RB = 32
CB = 128
RW = 16
CW = 256
FLAT = 289


def sigmoid(x):
    return 0.5 * jnp.tanh(0.5 * x) + 0.5


def store_shifted(x, dst, r, lane):
    z = jnp.zeros_like(x)
    dst[r, 0:CH] = jnp.where(lane == 0, z, pltpu.roll(x, 1, 1))
    dst[r, CH : 2 * CH] = x
    dst[r, 2 * CH : 3 * CH] = jnp.where(lane == CW - 1, z, pltpu.roll(x, CW - 1, 1))


def build_weights(w_ref, dst, transposed):
    dst[...] = jnp.zeros_like(dst)
    for a in range(3):
        for b in range(3):
            if transposed:
                block = w_ref[2 - a, 2 - b]
            else:
                block = w_ref[a, b].astype(F32).T.astype(BF)
            for t in range(2):
                first = (a + t) * 3 * CH + b * CH
                dst[t * CH : (t + 1) * CH, first : first + CH] = block


def conv(w, src, k):
    rhs = src[pl.ds(2 * k, 4)].reshape(4 * 3 * CH, CW)
    return jnp.dot(w[...], rhs, preferred_element_type=F32)


def kernel(
    n_sy,
    n_grp,
    scale,
    x_hbm,
    ct_hbm,
    w1_hbm,
    b1_hbm,
    w2_hbm,
    b2_hbm,
    out_ref,
    ig_ref,
    g1_ref,
    gb1_ref,
    g2_ref,
    gb2_ref,
    x_ref,
    ct_ref,
    w1_ref,
    b1_ref,
    w2_ref,
    b2_ref,
    turn,
    xt,
    ctt,
    xw,
    ctw,
    x3,
    h3,
    d3,
    e3,
    s1,
    dz,
    w1t,
    w2t,
    w1f,
    w2f,
    outw,
    igw,
    outs,
    igs,
    gacc,
    flat,
    part2,
    part1,
    in2,
    in1,
    mid2,
    mid1,
    fin2,
    fin1,
    send_halo,
    recv_halo,
    send_red,
    recv_red,
    load_sem,
):
    sy = lax.axis_index("sy")
    sx = lax.axis_index("sx")
    grp = lax.axis_index("grp")
    n_m = 2 * n_sy
    m = sy * 2 + sx
    chunk = part1.shape[1]

    loads = [
        pltpu.make_async_copy(src.at[part], dst.at[part], load_sem.at[i])
        for i, (src, dst, part) in enumerate(
            [(x_hbm, x_ref, pl.ds(16 * j, 16)) for j in range(4)]
            + [(ct_hbm, ct_ref, pl.ds(16 * j, 16)) for j in range(4)]
            + [(src, dst, pl.ds(0, src.shape[0])) for src, dst in (
                (w1_hbm, w1_ref), (w2_hbm, w2_ref), (b1_hbm, b1_ref), (b2_hbm, b2_ref))]
        )
    ]
    for load in loads:
        load.start()

    barrier = pltpu.get_barrier_semaphore()

    @pl.loop(1, n_m)
    def _(d):
        peer = lax.rem(m + d, n_m)
        pl.semaphore_signal(
            barrier,
            inc=1,
            device_id={"sy": peer // 2, "sx": lax.rem(peer, 2)},
            device_id_type=MESH,
        )

    @pl.loop(1, n_grp)
    def _(d):
        pl.semaphore_signal(
            barrier, inc=1, device_id={"grp": lax.rem(grp + d, n_grp)}, device_id_type=MESH
        )

    lane = lax.broadcasted_iota(jnp.int32, (CH, CW), 1)
    mine = pl.multiple_of(sx * CB, CB)
    other = pl.multiple_of((1 - sx) * CB, CB)

    def rows_major(first, src, dst):
        for j in range(4):
            loads[first + j].wait()
            part = src[16 * j : 16 * j + 16].astype(F32).reshape(16 * RB, CB)
            turn[16 * RB * j : 16 * RB * (j + 1)] = part

        @pl.loop(0, RB, unroll=RB)
        def _(r):
            dst[r] = turn[pl.ds(r, CH, stride=RB), :].astype(BF)

    has_down = sy < n_sy - 1
    has_up = sy > 0
    takes = ((sx == 0) & has_up) | ((sx == 1) & has_down)

    def halo_near(i, blk, win, width):
        return pltpu.make_async_copy(
            blk.at[pl.ds(sx * (RW - width), RW + width)],
            win.at[pl.ds((1 - sx) * width, RW + width), :, pl.ds(mine, CB)],
            send_halo.at[i, 0],
        )

    def halo_pair(i, blk, win, width):
        return pltpu.make_async_remote_copy(
            src_ref=blk.at[pl.ds((1 - sx) * (RW - width), RW + width)],
            dst_ref=win.at[pl.ds(sx * width, RW + width), :, pl.ds(mine, CB)],
            send_sem=send_halo.at[i, 1],
            recv_sem=recv_halo.at[i, 0],
            device_id={"sx": 1 - sx},
            device_id_type=MESH,
        )

    def halo_down(i, blk, win, width):
        return pltpu.make_async_remote_copy(
            src_ref=blk.at[pl.ds(RB - width, width)],
            dst_ref=win.at[pl.ds(0, width), :, pl.ds(mine, CB)],
            send_sem=send_halo.at[i, 2],
            recv_sem=recv_halo.at[i, 1 + sx],
            device_id={"sy": sy + 1, "sx": 0},
            device_id_type=MESH,
        )

    def halo_up(i, blk, win, width):
        return pltpu.make_async_remote_copy(
            src_ref=blk.at[pl.ds(0, width)],
            dst_ref=win.at[pl.ds(RW + width, width), :, pl.ds(mine, CB)],
            send_sem=send_halo.at[i, 3],
            recv_sem=recv_halo.at[i, 1 + sx],
            device_id={"sy": sy - 1, "sx": 1},
            device_id_type=MESH,
        )

    def halo_start(*what):
        _, _, win, width = what
        pl.when(has_down)(lambda: halo_down(*what).start())
        pl.when(has_up)(lambda: halo_up(*what).start())
        halo_pair(*what).start()
        halo_near(*what).start()
        empty = jnp.zeros((width, CH, CW), BF)

        @pl.when((sx == 0) & (sy == 0))
        def _():
            win[0:width] = empty

        @pl.when((sx == 1) & (sy == n_sy - 1))
        def _():
            win[RW + width : RW + 2 * width] = empty

    def halo_wait_pair(*what):
        halo_near(*what).wait()
        halo_pair(*what).wait()

    def halo_wait_far(*what):
        i, blk, win, width = what
        pl.when(has_down)(lambda: halo_down(*what).wait_send())
        pl.when(has_up)(lambda: halo_up(*what).wait_send())

        @pl.when(takes)
        def _():
            for half in range(2):
                pltpu.make_async_remote_copy(
                    src_ref=blk.at[pl.ds(0, width)],
                    dst_ref=win.at[
                        pl.ds(sx * (RW + width), width), :, half * CB : (half + 1) * CB
                    ],
                    send_sem=send_halo.at[i, 2],
                    recv_sem=recv_halo.at[i, 1 + half],
                    device_id={"sx": 1 - sx},
                    device_id_type=MESH,
                ).wait_recv()

    rows_major(0, x_ref, xt)
    pl.semaphore_wait(barrier, n_m - 1 + n_grp - 1)
    halo_start(0, xt, xw, 4)
    rows_major(4, ct_ref, ctt)
    halo_start(1, ctt, ctw, 2)

    for load in loads[8:]:
        load.wait()
    build_weights(w1_ref, w1t, False)
    build_weights(w2_ref, w2t, False)
    build_weights(w1_ref, w1f, True)
    build_weights(w2_ref, w2f, True)

    def column(ref):
        across_rows = jnp.broadcast_to(ref[...], (CH, CH))
        one = jnp.where(
            lax.broadcasted_iota(jnp.int32, (CH, CH), 0)
            == lax.broadcasted_iota(jnp.int32, (CH, CH), 1),
            across_rows,
            0.0,
        )
        col = jnp.broadcast_to(jnp.sum(one, axis=1, keepdims=True), (CH, CW))
        return jnp.concatenate([col, col], 0)

    b1 = column(b1_ref)
    b2 = column(b2_ref)
    blank = jnp.zeros((CH, CW), BF)
    first = (sx == 0) & (sy == 0)
    last = (sx == 1) & (sy == n_sy - 1)

    halo_wait_pair(0, xt, xw, 4)

    @pl.loop(0, RW + 4, unroll=RW + 4)
    def _(r):
        store_shifted(xw[r + 4 - 4 * sx], x3, r + 4 - 4 * sx, lane)

    def hidden_rows(k):
        pre = conv(w1t, x3, k) + b1
        gate = sigmoid(pre)
        h = (pre * gate).astype(BF)
        s1[pl.ds(2 * k, 2)] = (gate * (1.0 + pre * (1.0 - gate))).reshape(2, CH, CW)
        store_shifted(h[0:CH], h3, 2 * k, lane)
        store_shifted(h[CH : 2 * CH], h3, 2 * k + 1, lane)

    @pl.loop(0, (RW + 2) // 2, unroll=(RW + 2) // 2)
    def _(k):
        hidden_rows(k + 2 - 2 * sx)

    halo_wait_far(0, xt, xw, 4)

    @pl.loop(0, 4, unroll=4)
    def _(r):
        store_shifted(xw[r + (RW + 4) * sx], x3, r + (RW + 4) * sx, lane)

    @pl.loop(0, 2, unroll=2)
    def _(k):
        hidden_rows(k + (RW + 2) // 2 * sx)

    @pl.when(first)
    def _():
        h3[0:3] = jnp.zeros((3, 3 * CH, CW), BF)

    @pl.when(last)
    def _():
        h3[RW + 3 : RW + 6] = jnp.zeros((3, 3 * CH, CW), BF)

    halo_wait_pair(1, ctt, ctw, 2)
    halo_wait_far(1, ctt, ctw, 2)

    @pl.loop(0, (RW + 4) // 2, unroll=(RW + 4) // 2)
    def _(k):
        pre = conv(w2t, h3, k) + b2
        gate = sigmoid(pre)
        slope = gate * (1.0 + pre * (1.0 - gate))
        ct = ctw[pl.ds(2 * k, 2)].reshape(2 * CH, CW)
        d = (ct.astype(F32) * slope).astype(BF)
        store_shifted(d[0:CH], d3, 2 * k, lane)
        store_shifted(d[CH : 2 * CH], d3, 2 * k + 1, lane)

        outw[pl.ds(2 * k, 2)] = (pre * gate).astype(BF).reshape(2, CH, CW)
        dz[pl.ds(2 * k, 2)] = d.reshape(2, CH, CW)

    for r in (0, 1, RW + 2, RW + 3):
        dz[r] = blank

    def pair_copy(i, src, dst):
        return pltpu.make_async_remote_copy(
            src_ref=src.at[:, :, pl.ds(other, CB)],
            dst_ref=dst,
            send_sem=send_halo.at[2 + i, 0],
            recv_sem=recv_halo.at[2 + i, 0],
            device_id={"sx": 1 - sx},
            device_id_type=MESH,
        )

    pair_copy(0, outw.at[pl.ds(2, RW)], outs).start()

    def kernel_grad(src, off, dst):
        gacc[...] = jnp.zeros_like(gacc)
        ones = jnp.ones((16, CW), BF)

        @pl.loop(0, (RW + 2) // 2, unroll=(RW + 2) // 2)
        def _(k):
            q = 2 * k
            left = [jnp.concatenate([src[q + j + off], ones], 0) for j in range(2)]
            right = [dz[pl.ds(q + j, 3)].reshape(3 * CH, CW) for j in range(2)]
            gacc[...] += lax.dot_general(
                jnp.concatenate(left, 1),
                jnp.concatenate(right, 1),
                (((1,), (1,)), ((), ())),
                preferred_element_type=F32,
            )

        flat[0:192] = gacc[0:192, 0:128]
        tail = gacc[0:192, 128:192]
        flat[192:288] = jnp.concatenate([tail[0:96], tail[96:192]], 1)
        flat[288:289] = gacc[192:193, 0:128]
        for j in range(n_m):
            top = min(FLAT, (j + 1) * chunk)
            if top > j * chunk:
                dst[j, 0 : top - j * chunk] = flat[j * chunk : top]

    def peer_of(d):
        peer = lax.rem(m + d, n_m)
        return peer, {"sy": peer // 2, "sx": lax.rem(peer, 2)}

    def scatter(i, part, landing):
        def copy(d):
            peer, where = peer_of(d)
            return pltpu.make_async_remote_copy(
                src_ref=part.at[peer],
                dst_ref=landing.at[m],
                send_sem=send_red.at[i, d],
                recv_sem=recv_red.at[i, m],
                device_id=where,
                device_id_type=MESH,
            )

        return copy

    def across(i, mid):
        def copy(d):
            return pltpu.make_async_remote_copy(
                src_ref=mid.at[grp],
                dst_ref=mid.at[grp],
                send_sem=send_red.at[i, d],
                recv_sem=recv_red.at[i, grp],
                device_id={"grp": lax.rem(grp + d, n_grp)},
                device_id_type=MESH,
            )

        return copy

    def gather(i, fin):
        def copy(d):
            _, where = peer_of(d)
            return pltpu.make_async_remote_copy(
                src_ref=fin.at[m],
                dst_ref=fin.at[m],
                send_sem=send_red.at[i, d],
                recv_sem=recv_red.at[i, m],
                device_id=where,
                device_id_type=MESH,
            )

        return copy

    def start_all(copy, count):
        @pl.loop(1, count)
        def _(d):
            copy(d).start()

    def wait_all(copy, i, count, me, landing):
        @pl.loop(1, count)
        def _(d):
            slot = lax.rem(me + d, count)
            copy(d).wait_send()
            pltpu.make_async_remote_copy(
                src_ref=landing.at[slot],
                dst_ref=landing.at[slot],
                send_sem=send_red.at[i, d],
                recv_sem=recv_red.at[i, slot],
                device_id={"sx": 1 - sx},
                device_id_type=MESH,
            ).wait_recv()

    def total(landing, count):
        acc = landing[0]
        for j in range(1, count):
            acc = acc + landing[j]
        return acc

    def step_scatter(i, part, landing):
        landing[m] = part[m]
        start_all(scatter(i, part, landing), n_m)

    def step_across(i, part, landing, mid):
        wait_all(scatter(i, part, landing), i, n_m, m, landing)
        mid[grp] = total(landing, n_m)
        start_all(across(i + 1, mid), n_grp)

    def step_gather(i, mid, fin):
        wait_all(across(i + 1, mid), i + 1, n_grp, grp, mid)
        fin[m] = total(mid, n_grp)
        start_all(gather(i + 2, fin), n_m)

    def step_end(i, fin, g_out, gb_out):
        wait_all(gather(i + 2, fin), i + 2, n_m, m, fin)
        for j in range(n_m):
            top = min(FLAT, (j + 1) * chunk)
            if top > j * chunk:
                flat[j * chunk : top] = fin[j, 0 : top - j * chunk] * scale
        wide = flat[0:192]
        g_out[2] = wide[:, 0:64]
        g_out[1] = wide[:, 64:128]
        tail = flat[192:288]
        g_out[0, 0:96] = tail[:, 0:64]
        g_out[0, 96:192] = tail[:, 64:128]
        gb_out[...] = flat[288:289, 0:64]

    kernel_grad(h3, 2, part2)
    step_scatter(0, part2, in2)

    @pl.loop(0, (RW + 2) // 2, unroll=(RW + 2) // 2)
    def _(k):
        hg = conv(w2f, d3, k)
        d = (hg * s1[pl.ds(2 * k + 2, 2)].reshape(2 * CH, CW)).astype(BF)
        top, low = d[0:CH], d[CH : 2 * CH]
        store_shifted(top, e3, 2 * k, lane)
        store_shifted(low, e3, 2 * k + 1, lane)
        dz[2 * k + 1] = top
        dz[2 * k + 2] = low

    dz[1] = blank
    dz[RW + 2] = blank

    @pl.when(first)
    def _():
        e3[0] = jnp.zeros((3 * CH, CW), BF)

    @pl.when(last)
    def _():
        e3[RW + 1] = jnp.zeros((3 * CH, CW), BF)

    kernel_grad(x3, 3, part1)
    step_scatter(3, part1, in1)
    step_across(0, part2, in2, mid2)

    @pl.loop(0, RW // 2, unroll=RW // 2)
    def _(k):
        igw[pl.ds(2 * k, 2)] = conv(w1f, e3, k).astype(BF).reshape(2, CH, CW)

    pair_copy(1, igw, igs).start()
    step_across(3, part1, in1, mid1)
    step_gather(0, mid2, fin2)

    def channels_major(i, own, got, dst):
        pair_copy(i, own, got).wait()

        @pl.loop(0, RW, unroll=RW)
        def _(r):
            turn[pl.ds(sx * RW + r, CH, stride=RB), :] = own[r, :, pl.ds(mine, CB)].astype(F32)
            turn[pl.ds((1 - sx) * RW + r, CH, stride=RB), :] = got[r].astype(F32)

        @pl.loop(0, 8, unroll=8)
        def _(c):
            part = turn[pl.ds(pl.multiple_of(8 * RB * c, 8 * RB), 8 * RB)]
            dst[pl.ds(8 * c, 8)] = part.reshape(8, RB, CB).astype(BF)

    channels_major(0, outw.at[pl.ds(2, RW)], outs, out_ref)
    channels_major(1, igw, igs, ig_ref)
    step_gather(3, mid1, fin1)
    step_end(0, fin2, g2_ref, gb2_ref)
    step_end(3, fin1, g1_ref, gb1_ref)


def write_out(*refs):
    n = (len(refs) - 1) // 2
    copies = [
        pltpu.make_async_copy(refs[i], refs[n + i], refs[-1].at[i]) for i in range(n)
    ]
    for copy in copies:
        copy.start()
    for copy in copies:
        copy.wait()


def solution(mesh):
    n_sy = mesh.shape["sy"]
    n_grp = mesh.shape["grp"]
    n_m = 2 * n_sy
    chunk = -(-FLAT // n_m)
    scale = float((n_grp * n_sy * RB * 2 * CB) ** -0.5)
    most = max(n_m, n_grp)
    shapes = [
        jax.ShapeDtypeStruct((CH, RB, CB), BF),
        jax.ShapeDtypeStruct((CH, RB, CB), BF),
        jax.ShapeDtypeStruct((3, 3 * CH, CH), F32),
        jax.ShapeDtypeStruct((1, CH), F32),
        jax.ShapeDtypeStruct((3, 3 * CH, CH), F32),
        jax.ShapeDtypeStruct((1, CH), F32),
    ]
    call = pl.pallas_call(
        functools.partial(kernel, n_sy, n_grp, scale),
        out_shape=shapes,
        in_specs=[pl.BlockSpec(memory_space=pltpu.HBM)] * 6,
        out_specs=[pl.BlockSpec(memory_space=pltpu.VMEM)] * 6,
        scratch_shapes=[
            pltpu.VMEM((CH, RB, CB), BF),
            pltpu.VMEM((CH, RB, CB), BF),
            pltpu.VMEM((3, 3, CH, CH), BF),
            pltpu.VMEM((1, CH), F32),
            pltpu.VMEM((3, 3, CH, CH), BF),
            pltpu.VMEM((1, CH), F32),
            pltpu.VMEM((CH * RB, CB), F32),
            pltpu.VMEM((RB, CH, CB), BF),
            pltpu.VMEM((RB, CH, CB), BF),
            pltpu.VMEM((RW + 8, CH, CW), BF),
            pltpu.VMEM((RW + 4, CH, CW), BF),
            pltpu.VMEM((RW + 8, 3 * CH, CW), BF),
            pltpu.VMEM((RW + 6, 3 * CH, CW), BF),
            pltpu.VMEM((RW + 4, 3 * CH, CW), BF),
            pltpu.VMEM((RW + 2, 3 * CH, CW), BF),
            pltpu.VMEM((RW + 6, CH, CW), F32),
            pltpu.VMEM((RW + 4, CH, CW), BF),
            pltpu.VMEM((2 * CH, 12 * CH), BF),
            pltpu.VMEM((2 * CH, 12 * CH), BF),
            pltpu.VMEM((2 * CH, 12 * CH), BF),
            pltpu.VMEM((2 * CH, 12 * CH), BF),
            pltpu.VMEM((RW + 4, CH, CW), BF),
            pltpu.VMEM((RW, CH, CW), BF),
            pltpu.VMEM((RW, CH, CB), BF),
            pltpu.VMEM((RW, CH, CB), BF),
            pltpu.VMEM((208, 192), F32),
            pltpu.VMEM((FLAT, 128), F32),
            pltpu.VMEM((n_m, chunk, 128), F32),
            pltpu.VMEM((n_m, chunk, 128), F32),
            pltpu.VMEM((n_m, chunk, 128), F32),
            pltpu.VMEM((n_m, chunk, 128), F32),
            pltpu.VMEM((n_grp, chunk, 128), F32),
            pltpu.VMEM((n_grp, chunk, 128), F32),
            pltpu.VMEM((n_m, chunk, 128), F32),
            pltpu.VMEM((n_m, chunk, 128), F32),
            pltpu.SemaphoreType.DMA((4, 4)),
            pltpu.SemaphoreType.DMA((4, 3)),
            pltpu.SemaphoreType.DMA((6, most)),
            pltpu.SemaphoreType.DMA((6, most)),
            pltpu.SemaphoreType.DMA((12,)),
        ],
        compiler_params=pltpu.CompilerParams(
            collective_id=0, has_side_effects=True, vmem_limit_bytes=50 * 1024 * 1024
        ),
        name="blocks",
    )
    store = pl.pallas_call(
        write_out,
        out_shape=shapes,
        in_specs=[pl.BlockSpec(memory_space=pl.ANY)] * 6,
        out_specs=[pl.BlockSpec(memory_space=pltpu.HBM)] * 6,
        scratch_shapes=[pltpu.SemaphoreType.DMA((6,))],
        compiler_params=pltpu.CompilerParams(vmem_limit_bytes=1024 * 1024),
        name="write_out",
    )

    def local(image, weight_one, bias_one, weight_two, bias_two, cotangent):
        output, image_grad, g1, gb1, g2, gb2 = store(
            *call(
                *(
                    pltpu.with_memory_space_constraint(v, pltpu.HBM)
                    for v in (
                        image[0],
                        cotangent[0],
                        weight_one,
                        bias_one.reshape(1, CH),
                        weight_two,
                        bias_two.reshape(1, CH),
                    )
                )
            )
        )
        return (
            output[None],
            image_grad[None],
            g1.reshape(3, 3, CH, CH),
            gb1.reshape(CH),
            g2.reshape(3, 3, CH, CH),
            gb2.reshape(CH),
        )

    tile = P("grp", None, "sy", "sx")
    return jax.shard_map(
        local,
        mesh=mesh,
        in_specs=(tile, P(), P(), P(), P(), tile),
        out_specs=(tile, tile, P(), P(), P(), P()),
        check_vma=False,
    )
```

```python
import functools

import jax
import jax.numpy as jnp
from jax import lax
from jax.experimental import pallas as pl
from jax.experimental.pallas import tpu as pltpu
from jax.sharding import PartitionSpec as P

BF = jnp.bfloat16
F32 = jnp.float32
MESH = pl.DeviceIdType.MESH
CH = 64
RB = 32
CB = 128
RW = 16
CW = 256
FLAT = 296


def sigmoid(x):
    return 0.5 * jnp.tanh(0.5 * x) + 0.5


def store_shifted(x, dst, r, lane):
    z = jnp.zeros_like(x)
    dst[r, 0:CH] = jnp.where(lane == 0, z, pltpu.roll(x, 1, 1))
    dst[r, CH : 2 * CH] = x
    dst[r, 2 * CH : 3 * CH] = jnp.where(lane == CW - 1, z, pltpu.roll(x, CW - 1, 1))


def build_weights(w_ref, dst, transposed):
    dst[...] = jnp.zeros_like(dst)
    for a in range(3):
        for b in range(3):
            if transposed:
                block = w_ref[2 - a, 2 - b]
            else:
                block = w_ref[a, b].astype(F32).T.astype(BF)
            for t in range(2):
                first = (a + t) * 3 * CH + b * CH
                dst[t * CH : (t + 1) * CH, first : first + CH] = block


def conv(w, src, k):
    rhs = src[pl.ds(2 * k, 4)].reshape(4 * 3 * CH, CW)
    return jnp.dot(w[...], rhs, preferred_element_type=F32)


def kernel(
    n_sy,
    n_grp,
    scale,
    x_hbm,
    ct_hbm,
    w1_hbm,
    b1_hbm,
    w2_hbm,
    b2_hbm,
    out_ref,
    ig_ref,
    g1_ref,
    gb1_ref,
    g2_ref,
    gb2_ref,
    x_ref,
    ct_ref,
    w1_ref,
    b1_ref,
    w2_ref,
    b2_ref,
    turn,
    xt,
    ctt,
    xw,
    ctw,
    x3,
    h3,
    d3,
    e3,
    s1,
    dz2,
    dz1,
    w1t,
    w2t,
    w1f,
    w2f,
    outw,
    igw,
    outs,
    igs,
    gacc,
    flat,
    part,
    landed,
    mid,
    fin,
    send_halo,
    recv_halo,
    send_red,
    recv_red,
    load_sem,
):
    sy = lax.axis_index("sy")
    sx = lax.axis_index("sx")
    grp = lax.axis_index("grp")
    n_y = n_sy // 2
    n_a, n_b = 8 * n_y, n_grp // 2
    z, x_lo = grp // 2, lax.rem(grp, 2)
    a = ((sy // n_y * 2 + x_lo) * n_y + lax.rem(sy, n_y)) * 2 + sx
    b = z
    chunk = part.shape[1]

    loads = [
        pltpu.make_async_copy(src.at[piece], dst.at[piece], load_sem.at[i])
        for i, (src, dst, piece) in enumerate(
            [(x_hbm, x_ref, pl.ds(16 * j, 16)) for j in range(4)]
            + [(ct_hbm, ct_ref, pl.ds(16 * j, 16)) for j in range(4)]
            + [
                (src, dst, pl.ds(0, src.shape[0]))
                for src, dst in (
                    (w1_hbm, w1_ref),
                    (w2_hbm, w2_ref),
                    (b1_hbm, b1_ref),
                    (b2_hbm, b2_ref),
                )
            ]
        )
    ]
    for load in loads:
        load.start()

    def at_a(p):
        spot = p // 2
        x = spot // n_y
        return {
            "sy": x // 2 * n_y + lax.rem(spot, n_y),
            "sx": lax.rem(p, 2),
            "grp": z * 2 + lax.rem(x, 2),
        }

    def at_b(p):
        return {"grp": p * 2 + x_lo}

    has_down = sy < n_sy - 1
    has_up = sy > 0
    takes = ((sx == 0) & has_up) | ((sx == 1) & has_down)

    barrier = pltpu.get_barrier_semaphore()

    for d in range(1, n_b):
        pl.semaphore_signal(
            barrier, inc=1, device_id=at_b(lax.rem(b + d, n_b)), device_id_type=MESH
        )
    for d in range(1, n_a):
        pl.semaphore_signal(
            barrier, inc=1, device_id=at_a(lax.rem(a + d, n_a)), device_id_type=MESH
        )

    lane = lax.broadcasted_iota(jnp.int32, (CH, CW), 1)
    mine = pl.multiple_of(sx * CB, CB)
    other = pl.multiple_of((1 - sx) * CB, CB)

    def rows_major(first, src, dst):
        for j in range(4):
            loads[first + j].wait()
            part = src[16 * j : 16 * j + 16].astype(F32).reshape(16 * RB, CB)
            turn[16 * RB * j : 16 * RB * (j + 1)] = part

        @pl.loop(0, RB, unroll=RB)
        def _(r):
            dst[r] = turn[pl.ds(r, CH, stride=RB), :].astype(BF)

    def halo_near(i, blk, win, width):
        return pltpu.make_async_copy(
            blk.at[pl.ds(sx * (RW - width), RW + width)],
            win.at[pl.ds((1 - sx) * width, RW + width), :, pl.ds(mine, CB)],
            send_halo.at[i, 0],
        )

    def halo_pair(i, blk, win, width):
        return pltpu.make_async_remote_copy(
            src_ref=blk.at[pl.ds((1 - sx) * (RW - width), RW + width)],
            dst_ref=win.at[pl.ds(sx * width, RW + width), :, pl.ds(mine, CB)],
            send_sem=send_halo.at[i, 1],
            recv_sem=recv_halo.at[i, 0],
            device_id={"sx": 1 - sx},
            device_id_type=MESH,
        )

    def halo_down(i, blk, win, width):
        return pltpu.make_async_remote_copy(
            src_ref=blk.at[pl.ds(RB - width, width)],
            dst_ref=win.at[pl.ds(0, width), :, pl.ds(mine, CB)],
            send_sem=send_halo.at[i, 2],
            recv_sem=recv_halo.at[i, 1 + sx],
            device_id={"sy": sy + 1, "sx": 0},
            device_id_type=MESH,
        )

    def halo_up(i, blk, win, width):
        return pltpu.make_async_remote_copy(
            src_ref=blk.at[pl.ds(0, width)],
            dst_ref=win.at[pl.ds(RW + width, width), :, pl.ds(mine, CB)],
            send_sem=send_halo.at[i, 3],
            recv_sem=recv_halo.at[i, 1 + sx],
            device_id={"sy": sy - 1, "sx": 1},
            device_id_type=MESH,
        )

    def halo_start(*what):
        _, _, win, width = what
        pl.when(has_down)(lambda: halo_down(*what).start())
        pl.when(has_up)(lambda: halo_up(*what).start())
        halo_pair(*what).start()
        halo_near(*what).start()
        empty = jnp.zeros((width, CH, CW), BF)

        @pl.when((sx == 0) & (sy == 0))
        def _():
            win[0:width] = empty

        @pl.when((sx == 1) & (sy == n_sy - 1))
        def _():
            win[RW + width : RW + 2 * width] = empty

    def halo_wait_pair(*what):
        halo_near(*what).wait()
        halo_pair(*what).wait()

    def halo_wait_far(*what):
        i, blk, win, width = what
        pl.when(has_down)(lambda: halo_down(*what).wait_send())
        pl.when(has_up)(lambda: halo_up(*what).wait_send())

        @pl.when(takes)
        def _():
            for half in range(2):
                pltpu.make_async_remote_copy(
                    src_ref=blk.at[pl.ds(0, width)],
                    dst_ref=win.at[
                        pl.ds(sx * (RW + width), width), :, half * CB : (half + 1) * CB
                    ],
                    send_sem=send_halo.at[i, 2],
                    recv_sem=recv_halo.at[i, 1 + half],
                    device_id={"sx": 1 - sx},
                    device_id_type=MESH,
                ).wait_recv()

    rows_major(0, x_ref, xt)
    pl.semaphore_wait(barrier, n_a - 1 + n_b - 1)
    halo_start(0, xt, xw, 4)
    rows_major(4, ct_ref, ctt)
    halo_start(1, ctt, ctw, 2)

    for load in loads[8:]:
        load.wait()
    build_weights(w1_ref, w1t, False)
    build_weights(w2_ref, w2t, False)
    build_weights(w1_ref, w1f, True)
    build_weights(w2_ref, w2f, True)

    def column(ref):
        across_rows = jnp.broadcast_to(ref[...], (CH, CH))
        one = jnp.where(
            lax.broadcasted_iota(jnp.int32, (CH, CH), 0)
            == lax.broadcasted_iota(jnp.int32, (CH, CH), 1),
            across_rows,
            0.0,
        )
        col = jnp.broadcast_to(jnp.sum(one, axis=1, keepdims=True), (CH, CW))
        return jnp.concatenate([col, col], 0)

    b1 = column(b1_ref)
    b2 = column(b2_ref)
    blank = jnp.zeros((CH, CW), BF)
    first = (sx == 0) & (sy == 0)
    last = (sx == 1) & (sy == n_sy - 1)

    def each(count, body):
        pl.loop(0, count, unroll=count)(body)

    def hidden_rows(k):
        pre = conv(w1t, x3, k) + b1
        gate = sigmoid(pre)
        h = (pre * gate).astype(BF)
        s1[pl.ds(2 * k, 2)] = (gate * (1.0 + pre * (1.0 - gate))).reshape(2, CH, CW)
        store_shifted(h[0:CH], h3, 2 * k, lane)
        store_shifted(h[CH : 2 * CH], h3, 2 * k + 1, lane)

    def output_rows(k):
        pre = conv(w2t, h3, k) + b2
        gate = sigmoid(pre)
        slope = gate * (1.0 + pre * (1.0 - gate))
        ct = ctw[pl.ds(2 * k, 2)].reshape(2 * CH, CW)
        d = (ct.astype(F32) * slope).astype(BF)
        store_shifted(d[0:CH], d3, 2 * k, lane)
        store_shifted(d[CH : 2 * CH], d3, 2 * k + 1, lane)
        outw[pl.ds(2 * k, 2)] = (pre * gate).astype(BF).reshape(2, CH, CW)
        dz2[pl.ds(2 * k, 2)] = d.reshape(2, CH, CW)

    def delta_rows(k):
        hg = conv(w2f, d3, k)
        d = (hg * s1[pl.ds(2 * k + 2, 2)].reshape(2 * CH, CW)).astype(BF)
        top, low = d[0:CH], d[CH : 2 * CH]
        store_shifted(top, e3, 2 * k, lane)
        store_shifted(low, e3, 2 * k + 1, lane)
        dz1[2 * k + 1] = top
        dz1[2 * k + 2] = low

    halo_wait_pair(0, xt, xw, 4)
    each(RW + 4, lambda r: store_shifted(xw[r + 4 - 4 * sx], x3, r + 4 - 4 * sx, lane))
    each(RW // 2 + 1, lambda k: hidden_rows(k + 2 - 2 * sx))
    halo_wait_pair(1, ctt, ctw, 2)
    each(RW // 2, lambda k: output_rows(k + 2 - 2 * sx))
    each(RW // 2 - 1, lambda k: delta_rows(k + 2 - 2 * sx))

    halo_wait_far(0, xt, xw, 4)
    each(4, lambda r: store_shifted(xw[r + (RW + 4) * sx], x3, r + (RW + 4) * sx, lane))
    each(2, lambda k: hidden_rows(k + (RW // 2 + 1) * sx))

    @pl.when(first)
    def _():
        h3[0:3] = jnp.zeros((3, 3 * CH, CW), BF)

    @pl.when(last)
    def _():
        h3[RW + 3 : RW + 6] = jnp.zeros((3, 3 * CH, CW), BF)

    halo_wait_far(1, ctt, ctw, 2)
    each(2, lambda k: output_rows(k + RW // 2 * sx))
    each(2, lambda k: delta_rows(k + (RW // 2 - 1) * sx))

    @pl.when(first)
    def _():
        e3[0] = jnp.zeros((3 * CH, CW), BF)

    @pl.when(last)
    def _():
        e3[RW + 1] = jnp.zeros((3 * CH, CW), BF)

    for r in (0, 1, RW + 2, RW + 3):
        dz2[r] = blank
        dz1[r] = blank

    def pair_copy(i, src, dst):
        return pltpu.make_async_remote_copy(
            src_ref=src.at[:, :, pl.ds(other, CB)],
            dst_ref=dst,
            send_sem=send_halo.at[2 + i, 0],
            recv_sem=recv_halo.at[2 + i, 0],
            device_id={"sx": 1 - sx},
            device_id_type=MESH,
        )


    def kernel_grad(src, off, dz, base):
        gacc[...] = jnp.zeros_like(gacc)
        ones = jnp.ones((16, CW), BF)

        @pl.loop(0, (RW + 2) // 2, unroll=(RW + 2) // 2)
        def _(k):
            q = 2 * k
            left = [jnp.concatenate([src[q + j + off], ones], 0) for j in range(2)]
            right = [dz[pl.ds(q + j, 3)].reshape(3 * CH, CW) for j in range(2)]
            gacc[...] += lax.dot_general(
                jnp.concatenate(left, 1),
                jnp.concatenate(right, 1),
                (((1,), (1,)), ((), ())),
                preferred_element_type=F32,
            )

        flat[base : base + 192] = gacc[0:192, 0:128]
        tail = gacc[0:192, 128:192]
        flat[base + 192 : base + 288] = jnp.concatenate([tail[0:96], tail[96:192]], 1)
        flat[base + 288 : base + FLAT] = gacc[192:200, 0:128]

    def send_parts(i, count, me, where, source, landing):
        for d in range(1, count):
            p = lax.rem(me + d, count)
            pltpu.make_async_remote_copy(
                src_ref=source(p),
                dst_ref=landing.at[me],
                send_sem=send_red.at[i],
                recv_sem=recv_red.at[i],
                device_id=where(p),
                device_id_type=MESH,
            ).start()

    def wait_parts(i, count, landing):
        rest = landing.at[pl.ds(0, count - 1)]
        pltpu.make_async_remote_copy(
            src_ref=rest,
            dst_ref=rest,
            send_sem=send_red.at[i],
            recv_sem=recv_red.at[i],
            device_id={"sx": 1 - sx},
            device_id_type=MESH,
        ).wait()

    def total(landing, count):
        acc = landing[0]
        for j in range(1, count):
            acc = acc + landing[j]
        return acc

    def unpack(base, g_out, gb_out):
        wide = flat[base : base + 192]
        g_out[2] = wide[:, 0:64]
        g_out[1] = wide[:, 64:128]
        tail = flat[base + 192 : base + 288]
        g_out[0, 0:96] = tail[:, 0:64]
        g_out[0, 96:192] = tail[:, 64:128]
        gb_out[...] = flat[base + 288 : base + 289, 0:64]

    def channels_major(i, own, got, dst):
        pair_copy(i, own, got).wait()

        @pl.loop(0, RW, unroll=RW)
        def _(r):
            turn[pl.ds(sx * RW + r, CH, stride=RB), :] = own[r, :, pl.ds(mine, CB)].astype(F32)
            turn[pl.ds((1 - sx) * RW + r, CH, stride=RB), :] = got[r].astype(F32)

        @pl.loop(0, 8, unroll=8)
        def _(c):
            part = turn[pl.ds(pl.multiple_of(8 * RB * c, 8 * RB), 8 * RB)]
            dst[pl.ds(8 * c, 8)] = part.reshape(8, RB, CB).astype(BF)

    if n_a * chunk > 2 * FLAT:
        flat[2 * FLAT :] = jnp.zeros((n_a * chunk - 2 * FLAT, 128), F32)
    kernel_grad(x3, 3, dz1, 0)
    kernel_grad(h3, 2, dz2, FLAT)
    for j in range(n_a):
        part[j] = flat[j * chunk : (j + 1) * chunk]
    send_parts(0, n_a, a, at_a, lambda p: part.at[p], landed)
    landed[a] = part[a]
    pair_copy(0, outw.at[pl.ds(2, RW)], outs).start()

    @pl.loop(0, RW // 2, unroll=RW // 2)
    def _(k):
        igw[pl.ds(2 * k, 2)] = conv(w1f, e3, k).astype(BF).reshape(2, CH, CW)

    pair_copy(1, igw, igs).start()
    channels_major(0, outw.at[pl.ds(2, RW)], outs, out_ref)

    wait_parts(0, n_a, landed)
    mid[b] = total(landed, n_a)
    send_parts(1, n_b, b, at_b, lambda p: mid.at[b], mid)
    channels_major(1, igw, igs, ig_ref)

    wait_parts(1, n_b, mid)
    fin[a] = total(mid, n_b).astype(BF)
    send_parts(2, n_a, a, at_a, lambda p: fin.at[a], fin)
    wait_parts(2, n_a, fin)
    for j in range(n_a):
        flat[j * chunk : (j + 1) * chunk] = fin[j].astype(F32) * scale
    unpack(0, g1_ref, gb1_ref)
    unpack(FLAT, g2_ref, gb2_ref)


def write_out(*refs):
    n = (len(refs) - 1) // 2
    copies = [
        pltpu.make_async_copy(refs[i], refs[n + i], refs[-1].at[i]) for i in range(n)
    ]
    for copy in copies:
        copy.start()
    for copy in copies:
        copy.wait()


def solution(mesh):
    n_sy = mesh.shape["sy"]
    n_grp = mesh.shape["grp"]
    n_a, n_b = 4 * n_sy, n_grp // 2
    chunk = -(-2 * FLAT // (2 * n_a)) * 2
    scale = float((n_grp * n_sy * RB * 2 * CB) ** -0.5)
    shapes = [
        jax.ShapeDtypeStruct((CH, RB, CB), BF),
        jax.ShapeDtypeStruct((CH, RB, CB), BF),
        jax.ShapeDtypeStruct((3, 3 * CH, CH), F32),
        jax.ShapeDtypeStruct((1, CH), F32),
        jax.ShapeDtypeStruct((3, 3 * CH, CH), F32),
        jax.ShapeDtypeStruct((1, CH), F32),
    ]
    call = pl.pallas_call(
        functools.partial(kernel, n_sy, n_grp, scale),
        out_shape=shapes,
        in_specs=[pl.BlockSpec(memory_space=pltpu.HBM)] * 6,
        out_specs=[pl.BlockSpec(memory_space=pltpu.VMEM)] * 6,
        scratch_shapes=[
            pltpu.VMEM((CH, RB, CB), BF),
            pltpu.VMEM((CH, RB, CB), BF),
            pltpu.VMEM((3, 3, CH, CH), BF),
            pltpu.VMEM((1, CH), F32),
            pltpu.VMEM((3, 3, CH, CH), BF),
            pltpu.VMEM((1, CH), F32),
            pltpu.VMEM((CH * RB, CB), F32),
            pltpu.VMEM((RB, CH, CB), BF),
            pltpu.VMEM((RB, CH, CB), BF),
            pltpu.VMEM((RW + 8, CH, CW), BF),
            pltpu.VMEM((RW + 4, CH, CW), BF),
            pltpu.VMEM((RW + 8, 3 * CH, CW), BF),
            pltpu.VMEM((RW + 6, 3 * CH, CW), BF),
            pltpu.VMEM((RW + 4, 3 * CH, CW), BF),
            pltpu.VMEM((RW + 2, 3 * CH, CW), BF),
            pltpu.VMEM((RW + 6, CH, CW), F32),
            pltpu.VMEM((RW + 4, CH, CW), BF),
            pltpu.VMEM((RW + 4, CH, CW), BF),
            pltpu.VMEM((2 * CH, 12 * CH), BF),
            pltpu.VMEM((2 * CH, 12 * CH), BF),
            pltpu.VMEM((2 * CH, 12 * CH), BF),
            pltpu.VMEM((2 * CH, 12 * CH), BF),
            pltpu.VMEM((RW + 4, CH, CW), BF),
            pltpu.VMEM((RW, CH, CW), BF),
            pltpu.VMEM((RW, CH, CB), BF),
            pltpu.VMEM((RW, CH, CB), BF),
            pltpu.VMEM((208, 192), F32),
            pltpu.VMEM((n_a * chunk, 128), F32),
            pltpu.VMEM((n_a, chunk, 128), F32),
            pltpu.VMEM((n_a, chunk, 128), F32),
            pltpu.VMEM((n_b, chunk, 128), F32),
            pltpu.VMEM((n_a, chunk, 128), BF),
            pltpu.SemaphoreType.DMA((4, 4)),
            pltpu.SemaphoreType.DMA((4, 3)),
            pltpu.SemaphoreType.DMA((3,)),
            pltpu.SemaphoreType.DMA((3,)),
            pltpu.SemaphoreType.DMA((12,)),
        ],
        compiler_params=pltpu.CompilerParams(
            collective_id=0, has_side_effects=True, vmem_limit_bytes=50 * 1024 * 1024
        ),
        name="blocks",
    )
    store = pl.pallas_call(
        write_out,
        out_shape=shapes,
        in_specs=[pl.BlockSpec(memory_space=pl.ANY)] * 6,
        out_specs=[pl.BlockSpec(memory_space=pltpu.HBM)] * 6,
        scratch_shapes=[pltpu.SemaphoreType.DMA((6,))],
        compiler_params=pltpu.CompilerParams(vmem_limit_bytes=1024 * 1024),
        name="write_out",
    )

    def local(image, weight_one, bias_one, weight_two, bias_two, cotangent):
        output, image_grad, g1, gb1, g2, gb2 = store(
            *call(
                *(
                    pltpu.with_memory_space_constraint(v, pltpu.HBM)
                    for v in (
                        image[0],
                        cotangent[0],
                        weight_one,
                        bias_one.reshape(1, CH),
                        weight_two,
                        bias_two.reshape(1, CH),
                    )
                )
            )
        )
        return (
            output[None],
            image_grad[None],
            g1.reshape(3, 3, CH, CH),
            gb1.reshape(CH),
            g2.reshape(3, 3, CH, CH),
            gb2.reshape(CH),
        )

    tile = P("grp", None, "sy", "sx")
    return jax.shard_map(
        local,
        mesh=mesh,
        in_specs=(tile, P(), P(), P(), P(), tile),
        out_specs=(tile, tile, P(), P(), P(), P()),
        check_vma=False,
    )
```

```python
import functools

import jax
import jax.numpy as jnp
from jax import lax
from jax.experimental import pallas as pl
from jax.experimental.pallas import tpu as pltpu
from jax.sharding import PartitionSpec as P

BF = jnp.bfloat16
F32 = jnp.float32
MESH = pl.DeviceIdType.MESH
CH = 64
RB = 32
CB = 128
RW = 16
CW = 256
FLAT = 296


def sigmoid(x):
    return 0.5 * jnp.tanh(0.5 * x) + 0.5


def store_shifted(x, dst, r, lane):
    z = jnp.zeros_like(x)
    dst[r, 0:CH] = jnp.where(lane == 0, z, pltpu.roll(x, 1, 1))
    dst[r, CH : 2 * CH] = x
    dst[r, 2 * CH : 3 * CH] = jnp.where(lane == CW - 1, z, pltpu.roll(x, CW - 1, 1))


def build_weights(w_ref, dst, transposed):
    dst[...] = jnp.zeros_like(dst)
    for a in range(3):
        for b in range(3):
            if transposed:
                block = w_ref[2 - a, 2 - b]
            else:
                block = w_ref[a, b].astype(F32).T.astype(BF)
            for t in range(2):
                first = (a + t) * 3 * CH + b * CH
                dst[t * CH : (t + 1) * CH, first : first + CH] = block


def conv(w, src, k):
    rhs = src[pl.ds(2 * k, 4)].reshape(4 * 3 * CH, CW)
    return jnp.dot(w[...], rhs, preferred_element_type=F32)


def kernel(
    n_sy,
    n_grp,
    scale,
    x_hbm,
    ct_hbm,
    w1_hbm,
    b1_hbm,
    w2_hbm,
    b2_hbm,
    out_ref,
    ig_ref,
    g1_ref,
    gb1_ref,
    g2_ref,
    gb2_ref,
    x_ref,
    ct_ref,
    w1_ref,
    b1_ref,
    w2_ref,
    b2_ref,
    turn,
    xt,
    ctt,
    xw,
    ctw,
    x3,
    h3,
    d3,
    e3,
    s1,
    dz2,
    dz1,
    w1t,
    w2t,
    w1f,
    w2f,
    outw,
    igw,
    outs,
    igs,
    gacc,
    flat,
    part,
    landed,
    mid,
    fin,
    send_halo,
    recv_halo,
    send_red,
    recv_red,
    load_sem,
):
    sy = lax.axis_index("sy")
    sx = lax.axis_index("sx")
    grp = lax.axis_index("grp")
    n_y = n_sy // 2
    n_a, n_b = 8 * n_y, n_grp // 2
    z, x_lo = grp // 2, lax.rem(grp, 2)
    chunk = part.shape[1]

    loads = [
        pltpu.make_async_copy(src.at[piece], dst.at[piece], load_sem.at[i])
        for i, (src, dst, piece) in enumerate(
            [(x_hbm, x_ref, pl.ds(16 * j, 16)) for j in range(4)]
            + [(ct_hbm, ct_ref, pl.ds(16 * j, 16)) for j in range(4)]
            + [
                (src, dst, pl.ds(0, src.shape[0]))
                for src, dst in (
                    (w1_hbm, w1_ref),
                    (w2_hbm, w2_ref),
                    (b1_hbm, b1_ref),
                    (b2_hbm, b2_ref),
                )
            ]
        )
    ]
    for load in loads:
        load.start()

    x, y = sy // n_y * 2 + x_lo, lax.rem(sy, n_y)
    a, b = (x * n_y + y) * 2 + sx, z

    def ring(step, size):
        return min(step, size - step)

    offsets_a = [
        (dx, dy, dc) for dx in range(4) for dy in range(n_y) for dc in range(2) if dx + dy + dc
    ]
    offsets_a.sort(key=lambda o: -2 * ring(o[0], 4) - 2 * ring(o[1], n_y) - o[2])
    group_a = []
    for dx, dy, dc in offsets_a:
        px, py, pc = lax.rem(x + dx, 4), lax.rem(y + dy, n_y), lax.rem(sx + dc, 2)
        group_a.append(
            (
                (px * n_y + py) * 2 + pc,
                {"sy": px // 2 * n_y + py, "sx": pc, "grp": z * 2 + lax.rem(px, 2)},
            )
        )
    group_b = []
    for dz in sorted(range(1, n_b), key=lambda o: -ring(o, n_b)):
        pz = lax.rem(z + dz, n_b)
        group_b.append((pz, {"grp": pz * 2 + x_lo}))

    has_down = sy < n_sy - 1
    has_up = sy > 0
    takes = ((sx == 0) & has_up) | ((sx == 1) & has_down)

    barrier = pltpu.get_barrier_semaphore()

    for _, where in group_a + group_b:
        pl.semaphore_signal(barrier, inc=1, device_id=where, device_id_type=MESH)

    lane = lax.broadcasted_iota(jnp.int32, (CH, CW), 1)
    mine = pl.multiple_of(sx * CB, CB)
    other = pl.multiple_of((1 - sx) * CB, CB)

    def rows_major(first, src, dst):
        for j in range(4):
            loads[first + j].wait()
            part = src[16 * j : 16 * j + 16].astype(F32).reshape(16 * RB, CB)
            turn[16 * RB * j : 16 * RB * (j + 1)] = part

        @pl.loop(0, RB, unroll=RB)
        def _(r):
            dst[r] = turn[pl.ds(r, CH, stride=RB), :].astype(BF)

    def halo_near(i, blk, win, width):
        return pltpu.make_async_copy(
            blk.at[pl.ds(sx * (RW - width), RW + width)],
            win.at[pl.ds((1 - sx) * width, RW + width), :, pl.ds(mine, CB)],
            send_halo.at[i, 0],
        )

    def halo_pair(i, blk, win, width):
        return pltpu.make_async_remote_copy(
            src_ref=blk.at[pl.ds((1 - sx) * (RW - width), RW + width)],
            dst_ref=win.at[pl.ds(sx * width, RW + width), :, pl.ds(mine, CB)],
            send_sem=send_halo.at[i, 1],
            recv_sem=recv_halo.at[i, 0],
            device_id={"sx": 1 - sx},
            device_id_type=MESH,
        )

    def halo_down(i, blk, win, width):
        return pltpu.make_async_remote_copy(
            src_ref=blk.at[pl.ds(RB - width, width)],
            dst_ref=win.at[pl.ds(0, width), :, pl.ds(mine, CB)],
            send_sem=send_halo.at[i, 2],
            recv_sem=recv_halo.at[i, 1 + sx],
            device_id={"sy": sy + 1, "sx": 0},
            device_id_type=MESH,
        )

    def halo_up(i, blk, win, width):
        return pltpu.make_async_remote_copy(
            src_ref=blk.at[pl.ds(0, width)],
            dst_ref=win.at[pl.ds(RW + width, width), :, pl.ds(mine, CB)],
            send_sem=send_halo.at[i, 3],
            recv_sem=recv_halo.at[i, 1 + sx],
            device_id={"sy": sy - 1, "sx": 1},
            device_id_type=MESH,
        )

    def halo_start(*what):
        _, _, win, width = what
        pl.when(has_down)(lambda: halo_down(*what).start())
        pl.when(has_up)(lambda: halo_up(*what).start())
        halo_pair(*what).start()
        halo_near(*what).start()
        empty = jnp.zeros((width, CH, CW), BF)

        @pl.when((sx == 0) & (sy == 0))
        def _():
            win[0:width] = empty

        @pl.when((sx == 1) & (sy == n_sy - 1))
        def _():
            win[RW + width : RW + 2 * width] = empty

    def halo_wait_pair(*what):
        halo_near(*what).wait()
        halo_pair(*what).wait()

    def halo_wait_far(*what):
        i, blk, win, width = what
        pl.when(has_down)(lambda: halo_down(*what).wait_send())
        pl.when(has_up)(lambda: halo_up(*what).wait_send())

        @pl.when(takes)
        def _():
            for half in range(2):
                pltpu.make_async_remote_copy(
                    src_ref=blk.at[pl.ds(0, width)],
                    dst_ref=win.at[
                        pl.ds(sx * (RW + width), width), :, half * CB : (half + 1) * CB
                    ],
                    send_sem=send_halo.at[i, 2],
                    recv_sem=recv_halo.at[i, 1 + half],
                    device_id={"sx": 1 - sx},
                    device_id_type=MESH,
                ).wait_recv()

    rows_major(0, x_ref, xt)
    pl.semaphore_wait(barrier, n_a - 1 + n_b - 1)
    halo_start(0, xt, xw, 4)
    rows_major(4, ct_ref, ctt)
    halo_start(1, ctt, ctw, 2)

    for load in loads[8:]:
        load.wait()
    build_weights(w1_ref, w1t, False)
    build_weights(w2_ref, w2t, False)
    build_weights(w1_ref, w1f, True)
    build_weights(w2_ref, w2f, True)

    def column(ref):
        across_rows = jnp.broadcast_to(ref[...], (CH, CH))
        one = jnp.where(
            lax.broadcasted_iota(jnp.int32, (CH, CH), 0)
            == lax.broadcasted_iota(jnp.int32, (CH, CH), 1),
            across_rows,
            0.0,
        )
        col = jnp.broadcast_to(jnp.sum(one, axis=1, keepdims=True), (CH, CW))
        return jnp.concatenate([col, col], 0)

    b1 = column(b1_ref)
    b2 = column(b2_ref)
    blank = jnp.zeros((CH, CW), BF)
    first = (sx == 0) & (sy == 0)
    last = (sx == 1) & (sy == n_sy - 1)

    def each(count, body):
        pl.loop(0, count, unroll=count)(body)

    def hidden_rows(k):
        pre = conv(w1t, x3, k) + b1
        gate = sigmoid(pre)
        h = (pre * gate).astype(BF)
        s1[pl.ds(2 * k, 2)] = (gate * (1.0 + pre * (1.0 - gate))).reshape(2, CH, CW)
        store_shifted(h[0:CH], h3, 2 * k, lane)
        store_shifted(h[CH : 2 * CH], h3, 2 * k + 1, lane)

    def output_rows(k):
        pre = conv(w2t, h3, k) + b2
        gate = sigmoid(pre)
        slope = gate * (1.0 + pre * (1.0 - gate))
        ct = ctw[pl.ds(2 * k, 2)].reshape(2 * CH, CW)
        d = (ct.astype(F32) * slope).astype(BF)
        store_shifted(d[0:CH], d3, 2 * k, lane)
        store_shifted(d[CH : 2 * CH], d3, 2 * k + 1, lane)
        outw[pl.ds(2 * k, 2)] = (pre * gate).astype(BF).reshape(2, CH, CW)
        dz2[pl.ds(2 * k, 2)] = d.reshape(2, CH, CW)

    def delta_rows(k):
        hg = conv(w2f, d3, k)
        d = (hg * s1[pl.ds(2 * k + 2, 2)].reshape(2 * CH, CW)).astype(BF)
        top, low = d[0:CH], d[CH : 2 * CH]
        store_shifted(top, e3, 2 * k, lane)
        store_shifted(low, e3, 2 * k + 1, lane)
        dz1[2 * k + 1] = top
        dz1[2 * k + 2] = low

    halo_wait_pair(0, xt, xw, 4)
    each(RW + 4, lambda r: store_shifted(xw[r + 4 - 4 * sx], x3, r + 4 - 4 * sx, lane))
    each(RW // 2 + 1, lambda k: hidden_rows(k + 2 - 2 * sx))
    halo_wait_pair(1, ctt, ctw, 2)
    each(RW // 2, lambda k: output_rows(k + 2 - 2 * sx))
    each(RW // 2 - 1, lambda k: delta_rows(k + 2 - 2 * sx))

    halo_wait_far(0, xt, xw, 4)
    each(4, lambda r: store_shifted(xw[r + (RW + 4) * sx], x3, r + (RW + 4) * sx, lane))
    each(2, lambda k: hidden_rows(k + (RW // 2 + 1) * sx))

    @pl.when(first)
    def _():
        h3[0:3] = jnp.zeros((3, 3 * CH, CW), BF)

    @pl.when(last)
    def _():
        h3[RW + 3 : RW + 6] = jnp.zeros((3, 3 * CH, CW), BF)

    halo_wait_far(1, ctt, ctw, 2)
    each(2, lambda k: output_rows(k + RW // 2 * sx))
    each(2, lambda k: delta_rows(k + (RW // 2 - 1) * sx))

    @pl.when(first)
    def _():
        e3[0] = jnp.zeros((3 * CH, CW), BF)

    @pl.when(last)
    def _():
        e3[RW + 1] = jnp.zeros((3 * CH, CW), BF)

    for r in (0, 1, RW + 2, RW + 3):
        dz2[r] = blank
        dz1[r] = blank

    def pair_copy(i, src, dst):
        return pltpu.make_async_remote_copy(
            src_ref=src.at[:, :, pl.ds(other, CB)],
            dst_ref=dst,
            send_sem=send_halo.at[2 + i, 0],
            recv_sem=recv_halo.at[2 + i, 0],
            device_id={"sx": 1 - sx},
            device_id_type=MESH,
        )


    def kernel_grad(src, off, dz, base):
        gacc[...] = jnp.zeros_like(gacc)
        ones = jnp.ones((16, CW), BF)

        @pl.loop(0, (RW + 2) // 2, unroll=(RW + 2) // 2)
        def _(k):
            q = 2 * k
            left = [jnp.concatenate([src[q + j + off], ones], 0) for j in range(2)]
            right = [dz[pl.ds(q + j, 3)].reshape(3 * CH, CW) for j in range(2)]
            gacc[...] += lax.dot_general(
                jnp.concatenate(left, 1),
                jnp.concatenate(right, 1),
                (((1,), (1,)), ((), ())),
                preferred_element_type=F32,
            )

        flat[base : base + 192] = gacc[0:192, 0:128]
        tail = gacc[0:192, 128:192]
        flat[base + 192 : base + 288] = jnp.concatenate([tail[0:96], tail[96:192]], 1)
        flat[base + 288 : base + FLAT] = gacc[192:200, 0:128]

    def send_parts(i, group, me, source, landing):
        for p, where in group:
            pltpu.make_async_remote_copy(
                src_ref=source(p),
                dst_ref=landing.at[me],
                send_sem=send_red.at[i],
                recv_sem=recv_red.at[i],
                device_id=where,
                device_id_type=MESH,
            ).start()

    def wait_parts(i, count, landing):
        rest = landing.at[pl.ds(0, count - 1)]
        pltpu.make_async_remote_copy(
            src_ref=rest,
            dst_ref=rest,
            send_sem=send_red.at[i],
            recv_sem=recv_red.at[i],
            device_id={"sx": 1 - sx},
            device_id_type=MESH,
        ).wait()

    def total(landing, count):
        acc = landing[0]
        for j in range(1, count):
            acc = acc + landing[j]
        return acc

    def unpack(base, g_out, gb_out):
        wide = flat[base : base + 192]
        g_out[2] = wide[:, 0:64]
        g_out[1] = wide[:, 64:128]
        tail = flat[base + 192 : base + 288]
        g_out[0, 0:96] = tail[:, 0:64]
        g_out[0, 96:192] = tail[:, 64:128]
        gb_out[...] = flat[base + 288 : base + 289, 0:64]

    def channels_major(i, own, got, dst):
        pair_copy(i, own, got).wait()

        @pl.loop(0, RW, unroll=RW)
        def _(r):
            turn[pl.ds(sx * RW + r, CH, stride=RB), :] = own[r, :, pl.ds(mine, CB)].astype(F32)
            turn[pl.ds((1 - sx) * RW + r, CH, stride=RB), :] = got[r].astype(F32)

        @pl.loop(0, 8, unroll=8)
        def _(c):
            part = turn[pl.ds(pl.multiple_of(8 * RB * c, 8 * RB), 8 * RB)]
            dst[pl.ds(8 * c, 8)] = part.reshape(8, RB, CB).astype(BF)

    if n_a * chunk > 2 * FLAT:
        flat[2 * FLAT :] = jnp.zeros((n_a * chunk - 2 * FLAT, 128), F32)
    kernel_grad(x3, 3, dz1, 0)
    kernel_grad(h3, 2, dz2, FLAT)
    for j in range(n_a):
        part[j] = flat[j * chunk : (j + 1) * chunk]
    send_parts(0, group_a, a, lambda p: part.at[p], landed)
    landed[a] = part[a]
    pair_copy(0, outw.at[pl.ds(2, RW)], outs).start()

    @pl.loop(0, RW // 2, unroll=RW // 2)
    def _(k):
        igw[pl.ds(2 * k, 2)] = conv(w1f, e3, k).astype(BF).reshape(2, CH, CW)

    pair_copy(1, igw, igs).start()
    channels_major(0, outw.at[pl.ds(2, RW)], outs, out_ref)

    wait_parts(0, n_a, landed)
    mid[b] = total(landed, n_a)
    send_parts(1, group_b, b, lambda p: mid.at[b], mid)
    channels_major(1, igw, igs, ig_ref)

    wait_parts(1, n_b, mid)
    fin[a] = total(mid, n_b).astype(BF)
    send_parts(2, group_a, a, lambda p: fin.at[a], fin)
    wait_parts(2, n_a, fin)
    for j in range(n_a):
        flat[j * chunk : (j + 1) * chunk] = fin[j].astype(F32) * scale
    unpack(0, g1_ref, gb1_ref)
    unpack(FLAT, g2_ref, gb2_ref)


def write_out(*refs):
    n = (len(refs) - 1) // 2
    copies = [
        pltpu.make_async_copy(refs[i], refs[n + i], refs[-1].at[i]) for i in range(n)
    ]
    for copy in copies:
        copy.start()
    for copy in copies:
        copy.wait()


def solution(mesh):
    n_sy = mesh.shape["sy"]
    n_grp = mesh.shape["grp"]
    n_a, n_b = 4 * n_sy, n_grp // 2
    chunk = -(-2 * FLAT // (2 * n_a)) * 2
    scale = float((n_grp * n_sy * RB * 2 * CB) ** -0.5)
    shapes = [
        jax.ShapeDtypeStruct((CH, RB, CB), BF),
        jax.ShapeDtypeStruct((CH, RB, CB), BF),
        jax.ShapeDtypeStruct((3, 3 * CH, CH), F32),
        jax.ShapeDtypeStruct((1, CH), F32),
        jax.ShapeDtypeStruct((3, 3 * CH, CH), F32),
        jax.ShapeDtypeStruct((1, CH), F32),
    ]
    call = pl.pallas_call(
        functools.partial(kernel, n_sy, n_grp, scale),
        out_shape=shapes,
        in_specs=[pl.BlockSpec(memory_space=pltpu.HBM)] * 6,
        out_specs=[pl.BlockSpec(memory_space=pltpu.VMEM)] * 6,
        scratch_shapes=[
            pltpu.VMEM((CH, RB, CB), BF),
            pltpu.VMEM((CH, RB, CB), BF),
            pltpu.VMEM((3, 3, CH, CH), BF),
            pltpu.VMEM((1, CH), F32),
            pltpu.VMEM((3, 3, CH, CH), BF),
            pltpu.VMEM((1, CH), F32),
            pltpu.VMEM((CH * RB, CB), F32),
            pltpu.VMEM((RB, CH, CB), BF),
            pltpu.VMEM((RB, CH, CB), BF),
            pltpu.VMEM((RW + 8, CH, CW), BF),
            pltpu.VMEM((RW + 4, CH, CW), BF),
            pltpu.VMEM((RW + 8, 3 * CH, CW), BF),
            pltpu.VMEM((RW + 6, 3 * CH, CW), BF),
            pltpu.VMEM((RW + 4, 3 * CH, CW), BF),
            pltpu.VMEM((RW + 2, 3 * CH, CW), BF),
            pltpu.VMEM((RW + 6, CH, CW), F32),
            pltpu.VMEM((RW + 4, CH, CW), BF),
            pltpu.VMEM((RW + 4, CH, CW), BF),
            pltpu.VMEM((2 * CH, 12 * CH), BF),
            pltpu.VMEM((2 * CH, 12 * CH), BF),
            pltpu.VMEM((2 * CH, 12 * CH), BF),
            pltpu.VMEM((2 * CH, 12 * CH), BF),
            pltpu.VMEM((RW + 4, CH, CW), BF),
            pltpu.VMEM((RW, CH, CW), BF),
            pltpu.VMEM((RW, CH, CB), BF),
            pltpu.VMEM((RW, CH, CB), BF),
            pltpu.VMEM((208, 192), F32),
            pltpu.VMEM((n_a * chunk, 128), F32),
            pltpu.VMEM((n_a, chunk, 128), F32),
            pltpu.VMEM((n_a, chunk, 128), F32),
            pltpu.VMEM((n_b, chunk, 128), F32),
            pltpu.VMEM((n_a, chunk, 128), BF),
            pltpu.SemaphoreType.DMA((4, 4)),
            pltpu.SemaphoreType.DMA((4, 3)),
            pltpu.SemaphoreType.DMA((3,)),
            pltpu.SemaphoreType.DMA((3,)),
            pltpu.SemaphoreType.DMA((12,)),
        ],
        compiler_params=pltpu.CompilerParams(
            collective_id=0, has_side_effects=True, vmem_limit_bytes=50 * 1024 * 1024
        ),
        name="blocks",
    )
    store = pl.pallas_call(
        write_out,
        out_shape=shapes,
        in_specs=[pl.BlockSpec(memory_space=pl.ANY)] * 6,
        out_specs=[pl.BlockSpec(memory_space=pltpu.HBM)] * 6,
        scratch_shapes=[pltpu.SemaphoreType.DMA((6,))],
        compiler_params=pltpu.CompilerParams(vmem_limit_bytes=1024 * 1024),
        name="write_out",
    )

    def local(image, weight_one, bias_one, weight_two, bias_two, cotangent):
        output, image_grad, g1, gb1, g2, gb2 = store(
            *call(
                *(
                    pltpu.with_memory_space_constraint(v, pltpu.HBM)
                    for v in (
                        image[0],
                        cotangent[0],
                        weight_one,
                        bias_one.reshape(1, CH),
                        weight_two,
                        bias_two.reshape(1, CH),
                    )
                )
            )
        )
        return (
            output[None],
            image_grad[None],
            g1.reshape(3, 3, CH, CH),
            gb1.reshape(CH),
            g2.reshape(3, 3, CH, CH),
            gb2.reshape(CH),
        )

    tile = P("grp", None, "sy", "sx")
    return jax.shard_map(
        local,
        mesh=mesh,
        in_specs=(tile, P(), P(), P(), P(), tile),
        out_specs=(tile, tile, P(), P(), P(), P()),
        check_vma=False,
    )
```

```python
import functools

import jax
import jax.numpy as jnp
from jax import lax
from jax.experimental import pallas as pl
from jax.experimental.pallas import tpu as pltpu
from jax.sharding import PartitionSpec as P

BF = jnp.bfloat16
F32 = jnp.float32
MESH = pl.DeviceIdType.MESH
CH = 64
RB = 32
CB = 128
RW = 16
CW = 256
FLAT = 296


def sigmoid(x):
    return 0.5 * jnp.tanh(0.5 * x) + 0.5


def store_shifted(x, dst, r, lane):
    z = jnp.zeros_like(x)
    dst[r, 0:CH] = jnp.where(lane == 0, z, pltpu.roll(x, 1, 1))
    dst[r, CH : 2 * CH] = x
    dst[r, 2 * CH : 3 * CH] = jnp.where(lane == CW - 1, z, pltpu.roll(x, CW - 1, 1))


def build_weights(w_ref, dst, transposed):
    dst[...] = jnp.zeros_like(dst)
    for a in range(3):
        for b in range(3):
            if transposed:
                block = w_ref[2 - a, 2 - b]
            else:
                block = w_ref[a, b].astype(F32).T.astype(BF)
            for t in range(2):
                first = (a + t) * 3 * CH + b * CH
                dst[t * CH : (t + 1) * CH, first : first + CH] = block


def conv(w, src, k):
    rhs = src[pl.ds(2 * k, 4)].reshape(4 * 3 * CH, CW)
    return jnp.dot(w[...], rhs, preferred_element_type=F32)


def kernel(
    n_sy,
    n_grp,
    scale,
    x_hbm,
    ct_hbm,
    w1_hbm,
    b1_hbm,
    w2_hbm,
    b2_hbm,
    out_ref,
    ig_ref,
    g1_ref,
    gb1_ref,
    g2_ref,
    gb2_ref,
    x_ref,
    ct_ref,
    w1_ref,
    b1_ref,
    w2_ref,
    b2_ref,
    turn,
    xt,
    ctt,
    xw,
    ctw,
    x3,
    h3,
    d3,
    e3,
    s1,
    dz2,
    dz1,
    w1t,
    w2t,
    w1f,
    w2f,
    outw,
    igw,
    outs,
    igs,
    gacc,
    flat,
    part,
    landed,
    mid,
    fin,
    send_halo,
    recv_halo,
    send_red,
    recv_red,
    load_sem,
    entered,
):
    sy = lax.axis_index("sy")
    sx = lax.axis_index("sx")
    grp = lax.axis_index("grp")
    n_y = n_sy // 2
    n_a, n_b = 8 * n_y, n_grp // 2
    z, x_lo = grp // 2, lax.rem(grp, 2)
    chunk = part.shape[1]

    loads = [
        pltpu.make_async_copy(src.at[piece], dst.at[piece], load_sem.at[i])
        for i, (src, dst, piece) in enumerate(
            [(x_hbm, x_ref, pl.ds(16 * j, 16)) for j in range(4)]
            + [(ct_hbm, ct_ref, pl.ds(16 * j, 16)) for j in range(4)]
            + [
                (src, dst, pl.ds(0, src.shape[0]))
                for src, dst in (
                    (w1_hbm, w1_ref),
                    (w2_hbm, w2_ref),
                    (b1_hbm, b1_ref),
                    (b2_hbm, b2_ref),
                )
            ]
        )
    ]
    for load in loads:
        load.start()

    x, y = sy // n_y * 2 + x_lo, lax.rem(sy, n_y)
    a, b = (x * n_y + y) * 2 + sx, z

    def ring(step, size):
        return min(step, size - step)

    offsets_a = [
        (dx, dy, dc) for dx in range(4) for dy in range(n_y) for dc in range(2) if dx + dy + dc
    ]
    offsets_a.sort(key=lambda o: -2 * ring(o[0], 4) - 2 * ring(o[1], n_y) - o[2])
    group_a = []
    close = []
    for dx, dy, dc in offsets_a:
        px, py, pc = lax.rem(x + dx, 4), lax.rem(y + dy, n_y), lax.rem(sx + dc, 2)
        group_a.append(
            (
                (px * n_y + py) * 2 + pc,
                {"sy": px // 2 * n_y + py, "sx": pc, "grp": z * 2 + lax.rem(px, 2)},
            )
        )
        if ring(dx, 4) + ring(dy, n_y) <= 1:
            close.append(group_a[-1][1])
    group_b = []
    for dz in sorted(range(1, n_b), key=lambda o: -ring(o, n_b)):
        pz = lax.rem(z + dz, n_b)
        group_b.append((pz, {"grp": pz * 2 + x_lo}))
        if ring(dz, n_b) <= 1:
            close.append(group_b[-1][1])

    has_down = sy < n_sy - 1
    has_up = sy > 0
    takes = ((sx == 0) & has_up) | ((sx == 1) & has_down)

    barrier = pltpu.get_barrier_semaphore()

    for where in close:
        pl.semaphore_signal(barrier, inc=1, device_id=where, device_id_type=MESH)

    @pl.when(takes)
    def _():
        for core in range(2):
            pl.semaphore_signal(
                barrier,
                inc=1,
                device_id={"sy": sy - 1 + 2 * sx, "sx": core},
                device_id_type=MESH,
            )

    lane = lax.broadcasted_iota(jnp.int32, (CH, CW), 1)
    mine = pl.multiple_of(sx * CB, CB)
    other = pl.multiple_of((1 - sx) * CB, CB)

    def rows_major(first, src, dst):
        for j in range(4):
            loads[first + j].wait()
            part = src[16 * j : 16 * j + 16].astype(F32).reshape(16 * RB, CB)
            turn[16 * RB * j : 16 * RB * (j + 1)] = part

        @pl.loop(0, RB, unroll=RB)
        def _(r):
            dst[r] = turn[pl.ds(r, CH, stride=RB), :].astype(BF)

    def halo_near(i, blk, win, width):
        return pltpu.make_async_copy(
            blk.at[pl.ds(sx * (RW - width), RW + width)],
            win.at[pl.ds((1 - sx) * width, RW + width), :, pl.ds(mine, CB)],
            send_halo.at[i, 0],
        )

    def halo_pair(i, blk, win, width):
        return pltpu.make_async_remote_copy(
            src_ref=blk.at[pl.ds((1 - sx) * (RW - width), RW + width)],
            dst_ref=win.at[pl.ds(sx * width, RW + width), :, pl.ds(mine, CB)],
            send_sem=send_halo.at[i, 1],
            recv_sem=recv_halo.at[i, 0],
            device_id={"sx": 1 - sx},
            device_id_type=MESH,
        )

    def halo_down(i, blk, win, width):
        return pltpu.make_async_remote_copy(
            src_ref=blk.at[pl.ds(RB - width, width)],
            dst_ref=win.at[pl.ds(0, width), :, pl.ds(mine, CB)],
            send_sem=send_halo.at[i, 2],
            recv_sem=recv_halo.at[i, 1 + sx],
            device_id={"sy": sy + 1, "sx": 0},
            device_id_type=MESH,
        )

    def halo_up(i, blk, win, width):
        return pltpu.make_async_remote_copy(
            src_ref=blk.at[pl.ds(0, width)],
            dst_ref=win.at[pl.ds(RW + width, width), :, pl.ds(mine, CB)],
            send_sem=send_halo.at[i, 3],
            recv_sem=recv_halo.at[i, 1 + sx],
            device_id={"sy": sy - 1, "sx": 1},
            device_id_type=MESH,
        )

    def halo_start(*what):
        _, _, win, width = what
        pl.when(has_down)(lambda: halo_down(*what).start())
        pl.when(has_up)(lambda: halo_up(*what).start())
        halo_pair(*what).start()
        halo_near(*what).start()
        empty = jnp.zeros((width, CH, CW), BF)

        @pl.when((sx == 0) & (sy == 0))
        def _():
            win[0:width] = empty

        @pl.when((sx == 1) & (sy == n_sy - 1))
        def _():
            win[RW + width : RW + 2 * width] = empty

    def halo_wait_pair(*what):
        halo_near(*what).wait()
        halo_pair(*what).wait()

    def halo_wait_far(*what):
        i, blk, win, width = what
        pl.when(has_down)(lambda: halo_down(*what).wait_send())
        pl.when(has_up)(lambda: halo_up(*what).wait_send())

        @pl.when(takes)
        def _():
            for half in range(2):
                pltpu.make_async_remote_copy(
                    src_ref=blk.at[pl.ds(0, width)],
                    dst_ref=win.at[
                        pl.ds(sx * (RW + width), width), :, half * CB : (half + 1) * CB
                    ],
                    send_sem=send_halo.at[i, 2],
                    recv_sem=recv_halo.at[i, 1 + half],
                    device_id={"sx": 1 - sx},
                    device_id_type=MESH,
                ).wait_recv()

    rows_major(0, x_ref, xt)
    pl.semaphore_wait(
        barrier, len(close) + has_down.astype(jnp.int32) + has_up.astype(jnp.int32)
    )

    def tell(i):
        for where in close:
            pl.semaphore_signal(entered.at[i], inc=1, device_id=where, device_id_type=MESH)

    def hear(i):
        pl.semaphore_wait(entered.at[i], len(close))

    halo_start(0, xt, xw, 4)
    tell(0)
    rows_major(4, ct_ref, ctt)
    halo_start(1, ctt, ctw, 2)

    for load in loads[8:]:
        load.wait()
    build_weights(w1_ref, w1t, False)
    build_weights(w2_ref, w2t, False)
    build_weights(w1_ref, w1f, True)
    build_weights(w2_ref, w2f, True)

    def column(ref):
        across_rows = jnp.broadcast_to(ref[...], (CH, CH))
        one = jnp.where(
            lax.broadcasted_iota(jnp.int32, (CH, CH), 0)
            == lax.broadcasted_iota(jnp.int32, (CH, CH), 1),
            across_rows,
            0.0,
        )
        col = jnp.broadcast_to(jnp.sum(one, axis=1, keepdims=True), (CH, CW))
        return jnp.concatenate([col, col], 0)

    b1 = column(b1_ref)
    b2 = column(b2_ref)
    blank = jnp.zeros((CH, CW), BF)
    first = (sx == 0) & (sy == 0)
    last = (sx == 1) & (sy == n_sy - 1)

    def each(count, body):
        pl.loop(0, count, unroll=count)(body)

    def hidden_rows(k):
        pre = conv(w1t, x3, k) + b1
        gate = sigmoid(pre)
        h = (pre * gate).astype(BF)
        s1[pl.ds(2 * k, 2)] = (gate * (1.0 + pre * (1.0 - gate))).reshape(2, CH, CW)
        store_shifted(h[0:CH], h3, 2 * k, lane)
        store_shifted(h[CH : 2 * CH], h3, 2 * k + 1, lane)

    def output_rows(k):
        pre = conv(w2t, h3, k) + b2
        gate = sigmoid(pre)
        slope = gate * (1.0 + pre * (1.0 - gate))
        ct = ctw[pl.ds(2 * k, 2)].reshape(2 * CH, CW)
        d = (ct.astype(F32) * slope).astype(BF)
        store_shifted(d[0:CH], d3, 2 * k, lane)
        store_shifted(d[CH : 2 * CH], d3, 2 * k + 1, lane)
        outw[pl.ds(2 * k, 2)] = (pre * gate).astype(BF).reshape(2, CH, CW)
        dz2[pl.ds(2 * k, 2)] = d.reshape(2, CH, CW)

    def delta_rows(k):
        hg = conv(w2f, d3, k)
        d = (hg * s1[pl.ds(2 * k + 2, 2)].reshape(2 * CH, CW)).astype(BF)
        top, low = d[0:CH], d[CH : 2 * CH]
        store_shifted(top, e3, 2 * k, lane)
        store_shifted(low, e3, 2 * k + 1, lane)
        dz1[2 * k + 1] = top
        dz1[2 * k + 2] = low

    halo_wait_pair(0, xt, xw, 4)
    each(RW + 4, lambda r: store_shifted(xw[r + 4 - 4 * sx], x3, r + 4 - 4 * sx, lane))
    each(RW // 2 + 1, lambda k: hidden_rows(k + 2 - 2 * sx))
    hear(0)
    tell(1)
    halo_wait_pair(1, ctt, ctw, 2)
    each(RW // 2, lambda k: output_rows(k + 2 - 2 * sx))
    each(RW // 2 - 1, lambda k: delta_rows(k + 2 - 2 * sx))

    hear(1)
    tell(2)

    halo_wait_far(0, xt, xw, 4)
    each(4, lambda r: store_shifted(xw[r + (RW + 4) * sx], x3, r + (RW + 4) * sx, lane))
    each(2, lambda k: hidden_rows(k + (RW // 2 + 1) * sx))

    @pl.when(first)
    def _():
        h3[0:3] = jnp.zeros((3, 3 * CH, CW), BF)

    @pl.when(last)
    def _():
        h3[RW + 3 : RW + 6] = jnp.zeros((3, 3 * CH, CW), BF)

    halo_wait_far(1, ctt, ctw, 2)
    each(2, lambda k: output_rows(k + RW // 2 * sx))
    each(2, lambda k: delta_rows(k + (RW // 2 - 1) * sx))

    @pl.when(first)
    def _():
        e3[0] = jnp.zeros((3 * CH, CW), BF)

    @pl.when(last)
    def _():
        e3[RW + 1] = jnp.zeros((3 * CH, CW), BF)

    for r in (0, 1, RW + 2, RW + 3):
        dz2[r] = blank
        dz1[r] = blank

    def pair_copy(i, src, dst):
        return pltpu.make_async_remote_copy(
            src_ref=src.at[:, :, pl.ds(other, CB)],
            dst_ref=dst,
            send_sem=send_halo.at[2 + i, 0],
            recv_sem=recv_halo.at[2 + i, 0],
            device_id={"sx": 1 - sx},
            device_id_type=MESH,
        )


    def kernel_grad(src, off, dz, base):
        gacc[...] = jnp.zeros_like(gacc)
        ones = jnp.ones((16, CW), BF)

        @pl.loop(0, (RW + 2) // 2, unroll=(RW + 2) // 2)
        def _(k):
            q = 2 * k
            left = [jnp.concatenate([src[q + j + off], ones], 0) for j in range(2)]
            right = [dz[pl.ds(q + j, 3)].reshape(3 * CH, CW) for j in range(2)]
            gacc[...] += lax.dot_general(
                jnp.concatenate(left, 1),
                jnp.concatenate(right, 1),
                (((1,), (1,)), ((), ())),
                preferred_element_type=F32,
            )

        flat[base : base + 192] = gacc[0:192, 0:128]
        tail = gacc[0:192, 128:192]
        flat[base + 192 : base + 288] = jnp.concatenate([tail[0:96], tail[96:192]], 1)
        flat[base + 288 : base + FLAT] = gacc[192:200, 0:128]

    def send_parts(i, group, me, source, landing):
        for p, where in group:
            pltpu.make_async_remote_copy(
                src_ref=source(p),
                dst_ref=landing.at[me],
                send_sem=send_red.at[i],
                recv_sem=recv_red.at[i],
                device_id=where,
                device_id_type=MESH,
            ).start()

    def wait_parts(i, count, landing):
        rest = landing.at[pl.ds(0, count - 1)]
        pltpu.make_async_remote_copy(
            src_ref=rest,
            dst_ref=rest,
            send_sem=send_red.at[i],
            recv_sem=recv_red.at[i],
            device_id={"sx": 1 - sx},
            device_id_type=MESH,
        ).wait()

    def total(landing, count):
        acc = landing[0]
        for j in range(1, count):
            acc = acc + landing[j]
        return acc

    def unpack(base, g_out, gb_out):
        wide = flat[base : base + 192]
        g_out[2] = wide[:, 0:64]
        g_out[1] = wide[:, 64:128]
        tail = flat[base + 192 : base + 288]
        g_out[0, 0:96] = tail[:, 0:64]
        g_out[0, 96:192] = tail[:, 64:128]
        gb_out[...] = flat[base + 288 : base + 289, 0:64]

    def channels_major(i, own, got, dst):
        pair_copy(i, own, got).wait()

        @pl.loop(0, RW, unroll=RW)
        def _(r):
            turn[pl.ds(sx * RW + r, CH, stride=RB), :] = own[r, :, pl.ds(mine, CB)].astype(F32)
            turn[pl.ds((1 - sx) * RW + r, CH, stride=RB), :] = got[r].astype(F32)

        @pl.loop(0, 8, unroll=8)
        def _(c):
            part = turn[pl.ds(pl.multiple_of(8 * RB * c, 8 * RB), 8 * RB)]
            dst[pl.ds(8 * c, 8)] = part.reshape(8, RB, CB).astype(BF)

    if n_a * chunk > 2 * FLAT:
        flat[2 * FLAT :] = jnp.zeros((n_a * chunk - 2 * FLAT, 128), F32)
    kernel_grad(x3, 3, dz1, 0)
    kernel_grad(h3, 2, dz2, FLAT)
    for j in range(n_a):
        part[j] = flat[j * chunk : (j + 1) * chunk]
    hear(2)
    send_parts(0, group_a, a, lambda p: part.at[p], landed)
    landed[a] = part[a]
    pair_copy(0, outw.at[pl.ds(2, RW)], outs).start()

    @pl.loop(0, RW // 2, unroll=RW // 2)
    def _(k):
        igw[pl.ds(2 * k, 2)] = conv(w1f, e3, k).astype(BF).reshape(2, CH, CW)

    pair_copy(1, igw, igs).start()
    channels_major(0, outw.at[pl.ds(2, RW)], outs, out_ref)

    wait_parts(0, n_a, landed)
    mid[b] = total(landed, n_a)
    send_parts(1, group_b, b, lambda p: mid.at[b], mid)
    channels_major(1, igw, igs, ig_ref)

    wait_parts(1, n_b, mid)
    fin[a] = total(mid, n_b).astype(BF)
    send_parts(2, group_a, a, lambda p: fin.at[a], fin)
    wait_parts(2, n_a, fin)
    for j in range(n_a):
        flat[j * chunk : (j + 1) * chunk] = fin[j].astype(F32) * scale
    unpack(0, g1_ref, gb1_ref)
    unpack(FLAT, g2_ref, gb2_ref)


def write_out(*refs):
    n = (len(refs) - 1) // 2
    copies = [
        pltpu.make_async_copy(refs[i], refs[n + i], refs[-1].at[i]) for i in range(n)
    ]
    for copy in copies:
        copy.start()
    for copy in copies:
        copy.wait()


def solution(mesh):
    n_sy = mesh.shape["sy"]
    n_grp = mesh.shape["grp"]
    n_a, n_b = 4 * n_sy, n_grp // 2
    chunk = -(-2 * FLAT // (2 * n_a)) * 2
    scale = float((n_grp * n_sy * RB * 2 * CB) ** -0.5)
    shapes = [
        jax.ShapeDtypeStruct((CH, RB, CB), BF),
        jax.ShapeDtypeStruct((CH, RB, CB), BF),
        jax.ShapeDtypeStruct((3, 3 * CH, CH), F32),
        jax.ShapeDtypeStruct((1, CH), F32),
        jax.ShapeDtypeStruct((3, 3 * CH, CH), F32),
        jax.ShapeDtypeStruct((1, CH), F32),
    ]
    call = pl.pallas_call(
        functools.partial(kernel, n_sy, n_grp, scale),
        out_shape=shapes,
        in_specs=[pl.BlockSpec(memory_space=pltpu.HBM)] * 6,
        out_specs=[pl.BlockSpec(memory_space=pltpu.VMEM)] * 6,
        scratch_shapes=[
            pltpu.VMEM((CH, RB, CB), BF),
            pltpu.VMEM((CH, RB, CB), BF),
            pltpu.VMEM((3, 3, CH, CH), BF),
            pltpu.VMEM((1, CH), F32),
            pltpu.VMEM((3, 3, CH, CH), BF),
            pltpu.VMEM((1, CH), F32),
            pltpu.VMEM((CH * RB, CB), F32),
            pltpu.VMEM((RB, CH, CB), BF),
            pltpu.VMEM((RB, CH, CB), BF),
            pltpu.VMEM((RW + 8, CH, CW), BF),
            pltpu.VMEM((RW + 4, CH, CW), BF),
            pltpu.VMEM((RW + 8, 3 * CH, CW), BF),
            pltpu.VMEM((RW + 6, 3 * CH, CW), BF),
            pltpu.VMEM((RW + 4, 3 * CH, CW), BF),
            pltpu.VMEM((RW + 2, 3 * CH, CW), BF),
            pltpu.VMEM((RW + 6, CH, CW), F32),
            pltpu.VMEM((RW + 4, CH, CW), BF),
            pltpu.VMEM((RW + 4, CH, CW), BF),
            pltpu.VMEM((2 * CH, 12 * CH), BF),
            pltpu.VMEM((2 * CH, 12 * CH), BF),
            pltpu.VMEM((2 * CH, 12 * CH), BF),
            pltpu.VMEM((2 * CH, 12 * CH), BF),
            pltpu.VMEM((RW + 4, CH, CW), BF),
            pltpu.VMEM((RW, CH, CW), BF),
            pltpu.VMEM((RW, CH, CB), BF),
            pltpu.VMEM((RW, CH, CB), BF),
            pltpu.VMEM((208, 192), F32),
            pltpu.VMEM((n_a * chunk, 128), F32),
            pltpu.VMEM((n_a, chunk, 128), F32),
            pltpu.VMEM((n_a, chunk, 128), F32),
            pltpu.VMEM((n_b, chunk, 128), F32),
            pltpu.VMEM((n_a, chunk, 128), BF),
            pltpu.SemaphoreType.DMA((4, 4)),
            pltpu.SemaphoreType.DMA((4, 3)),
            pltpu.SemaphoreType.DMA((3,)),
            pltpu.SemaphoreType.DMA((3,)),
            pltpu.SemaphoreType.DMA((12,)),
            pltpu.SemaphoreType.REGULAR((3,)),
        ],
        compiler_params=pltpu.CompilerParams(
            collective_id=0, has_side_effects=True, vmem_limit_bytes=50 * 1024 * 1024
        ),
        name="blocks",
    )
    store = pl.pallas_call(
        write_out,
        out_shape=shapes,
        in_specs=[pl.BlockSpec(memory_space=pl.ANY)] * 6,
        out_specs=[pl.BlockSpec(memory_space=pltpu.HBM)] * 6,
        scratch_shapes=[pltpu.SemaphoreType.DMA((6,))],
        compiler_params=pltpu.CompilerParams(vmem_limit_bytes=1024 * 1024),
        name="write_out",
    )

    def local(image, weight_one, bias_one, weight_two, bias_two, cotangent):
        output, image_grad, g1, gb1, g2, gb2 = store(
            *call(
                *(
                    pltpu.with_memory_space_constraint(v, pltpu.HBM)
                    for v in (
                        image[0],
                        cotangent[0],
                        weight_one,
                        bias_one.reshape(1, CH),
                        weight_two,
                        bias_two.reshape(1, CH),
                    )
                )
            )
        )
        return (
            output[None],
            image_grad[None],
            g1.reshape(3, 3, CH, CH),
            gb1.reshape(CH),
            g2.reshape(3, 3, CH, CH),
            gb2.reshape(CH),
        )

    tile = P("grp", None, "sy", "sx")
    return jax.shard_map(
        local,
        mesh=mesh,
        in_specs=(tile, P(), P(), P(), P(), tile),
        out_specs=(tile, tile, P(), P(), P(), P()),
        check_vma=False,
    )
```
